32 devices in a mesh: team: 2 (over core), obs: 4 (over z), grid: 4 (over y, x).
Axes of the slice: x: 2, y: 2, z: 4, core: 2. Of those that a mesh axis runs over, the one named last changes fastest.
Arguments:
- design_panel: bfloat16 [8192, 1024], P('obs', ('team', 'grid')), may hold values from -6 to 6
- design_front: bfloat16 [8192, 6144], P('obs', 'grid'), may hold values from -6 to 6
- arc_ids: int32 [8192], P('obs'), may hold values from 0 to 127
- arc_weight: float32 [128], replicated, may hold values from 0.5 to 2
- row_counts: int32 [4], P('obs'), may hold values from 128 to 2048, as said below
- panel_inverse: float32 [1024, 1024], P(('team', 'obs')), may hold values from -6.525546e-05 to 0.0020539933
- front: float32 [6144, 6144], P(('team', 'obs'), 'grid'), may hold values from -1.2 to 21.2
Outputs:
- factor_row: float32 [1024, 6144], P(('team', 'obs'), 'grid')
- front_next: float32 [6144, 6144], P(('team', 'obs'), 'grid')
The draws below stay inside these ranges and needn't reach their ends.
Inputs may be any that keep to these rules, and one draw needn't show every extreme that they name: `row_counts`: every count is a multiple of 128, and in every draw some shard's count equals 2048.
All inputs are finite; a program needn't handle non-finite values.
Results may differ from the reference program's by a relative error of at most 0.0035.
Values may be sent and summed in bfloat16 or wider, within the bound.
A program may use at most 64 MiB of HBM per device.

```python
import math
import jax
import jax.numpy as jnp
from jax import lax

B = 1024
M2 = 6144
ROW_DEV = 2048
ARCS = 128
SHARDS = 4
OBS_ROWS = 8192


def draw_row_counts(key, part):
    tiles_most = ROW_DEV // 128
    key_tiles, key_peak = jax.random.split(jax.random.fold_in(key, 11))
    picked = jax.random.randint(key_tiles, (SHARDS,), 1, tiles_most + 1)
    tile_counts = jnp.maximum(picked * picked // tiles_most, 1)
    peak_shard = jax.random.randint(key_peak, (), 0, SHARDS)
    tile_counts = jnp.where(jnp.arange(SHARDS) == peak_shard, tiles_most, tile_counts)
    return (tile_counts * 128).astype(jnp.int32)


def draw_panel_inverse(key, part):
    key_diag, key_off = jax.random.split(jax.random.fold_in(key, 23))
    overall = 0.09 / jnp.sqrt(jnp.float32(OBS_ROWS))
    diagonal = jax.random.uniform(key_diag, (B,), jnp.float32, 1.0, 2.0)
    off_diagonal = 0.7 * jnp.clip(jax.random.normal(key_off, (B, B), jnp.float32), -3.0, 3.0) / jnp.sqrt(jnp.float32(B))
    lower = jnp.tril(jnp.ones((B, B), jnp.float32), -1)
    return overall * (off_diagonal * lower + jnp.diag(diagonal))


def draw_front(key, part):
    key_sym, key_diag = jax.random.split(jax.random.fold_in(key, 37))
    noise_draw = jnp.clip(jax.random.normal(key_sym, (M2, M2), jnp.float32), -4.0, 4.0)
    symmetric = 0.15 * (noise_draw + noise_draw.T)
    diagonal = jax.random.uniform(key_diag, (M2,), jnp.float32, 12.0, 20.0)
    return symmetric + jnp.diag(diagonal)


def set_ends(values, key, least, largest):
    spot = [jax.random.randint(jax.random.fold_in(key, axis), (), 0, length) for axis, length in enumerate(values.shape)]
    main_axis = values.shape.index(max(values.shape))
    beside = spot[:main_axis] + [(spot[main_axis] + 1) % values.shape[main_axis]] + spot[main_axis + 1:]
    return values.at[tuple(spot)].set(least).at[tuple(beside)].set(largest)


def shard_levels(rng, dims, shards, low, high):
    factor_of = 1.0
    for dim, parts in shards:
        draws = jax.random.uniform(jax.random.fold_in(jax.random.fold_in(rng, 6), dim), (parts,), jnp.float32, low / len(shards), high / len(shards))
        factor_of = factor_of * jnp.repeat(jnp.exp(draws), dims[dim] // parts).reshape((-1,) + (1,) * (len(dims) - 1 - dim))
    return factor_of


def bell_draw(own_key, extent, spread, limit, cuts=(), kind=jnp.bfloat16):
    loudness = shard_levels(own_key, extent, cuts, -0.22, 0.18) if cuts else 1.0
    entries = jax.random.normal(own_key, extent, jnp.float32) * spread * loudness
    return jnp.minimum(jnp.maximum(entries, -limit), limit).astype(kind)


def setup_inputs(seed: int = 0) -> dict:
    key_list = jax.random.split(jax.random.key(seed), 8)
    return {
        "design_panel": bell_draw(key_list[0], (OBS_ROWS, B), 1.0, 6.0, ((0, 4), (1, 8))),
        "design_front": bell_draw(key_list[1], (OBS_ROWS, M2), 1.0, 6.0, ((0, 4), (1, 4))),
        "arc_ids": set_ends(jax.random.randint(key_list[2], (OBS_ROWS,), 0, ARCS), jax.random.fold_in(key_list[2], 1), 0, ARCS - 1).astype(jnp.int32),
        "arc_weight": jnp.clip(jnp.exp(jax.random.uniform(key_list[3], (ARCS,), jnp.float32, math.log(0.5), math.log(2.0))), 0.5, 2.0),
        "row_counts": draw_row_counts(jax.random.fold_in(key_list[7], 71), 0),
        "panel_inverse": draw_panel_inverse(jax.random.fold_in(key_list[7], 71), 0),
        "front": draw_front(jax.random.fold_in(key_list[7], 71), 0),
    }


def reference(design_panel, design_front, arc_ids, arc_weight, row_counts, panel_inverse, front):
    position = jnp.arange(OBS_ROWS, dtype=jnp.int32)
    shard_of = (position // ROW_DEV).astype(jnp.int32)
    within = (position % ROW_DEV).astype(jnp.int32)
    is_live = (within < row_counts[shard_of]).astype(jnp.float32)
    row_weight = arc_weight[arc_ids] * is_live
    panel_shards = design_panel.reshape(SHARDS, ROW_DEV, B)
    front_shards = design_front.reshape(SHARDS, ROW_DEV, M2)
    weight_shards = row_weight.reshape(SHARDS, ROW_DEV)

    def add_shard(running, pieces):
        panel_piece, front_piece, weight_piece = pieces
        scaled_rows = (front_piece.astype(jnp.float32) * weight_piece[:, None]).astype(jnp.bfloat16)
        return running + jnp.dot(panel_piece.T, scaled_rows, preferred_element_type=jnp.float32), None

    panel_block = lax.scan(add_shard, jnp.zeros((B, M2), jnp.float32), (panel_shards, front_shards, weight_shards))[0]
    factor_row = jnp.dot(panel_inverse, panel_block, precision=lax.Precision.HIGHEST, preferred_element_type=jnp.float32)
    update = jnp.dot(factor_row.T, factor_row, precision=lax.Precision.HIGHEST, preferred_element_type=jnp.float32)
    return factor_row, front - update
```

```python
import functools

import jax
import jax.numpy as jnp
from jax import lax
from jax.experimental import pallas as pl
from jax.experimental.pallas import tpu as pltpu
from jax.sharding import PartitionSpec as P


def live_weights(arc_ids, arc_weight, row_counts):
    row_total = arc_ids.shape[0]
    arc_total = arc_weight.shape[0]
    hit = arc_ids[:, None] == lax.broadcasted_iota(jnp.int32, (row_total, arc_total), 1)
    looked = jnp.sum(jnp.where(hit, arc_weight[None, :], 0.0), axis=1)
    is_live = lax.broadcasted_iota(jnp.int32, (row_total,), 0) < row_counts[0]
    return looked * is_live.astype(jnp.float32)


def contract_rows(left, right):
    return lax.dot_general(
        left, right, (((0,), (0,)), ((), ())), preferred_element_type=jnp.float32
    )


def local(design_panel, design_front, arc_ids, arc_weight, row_counts, panel_inverse, front):
    high = lax.reduce_precision(panel_inverse, 8, 7)
    split = jnp.concatenate([high, panel_inverse - high], axis=1).astype(jnp.bfloat16)
    inverse_whole = lax.all_gather(split, ("team", "obs"), axis=0, tiled=True)
    weights = live_weights(arc_ids, arc_weight, row_counts)
    scaled_front = (design_front.astype(jnp.float32) * weights[:, None]).astype(jnp.bfloat16)
    panel_piece = lax.all_gather(design_panel, "grid", axis=1, tiled=True)
    partial_value = contract_rows(panel_piece, scaled_front)
    slab_rows = panel_inverse.shape[0]
    place_index = lax.axis_index(("team", "obs"))
    block_part = lax.psum_scatter(partial_value, "obs", scatter_dimension=0, tiled=True)
    block_part = block_part.astype(jnp.bfloat16)
    block_whole = lax.all_gather(block_part, ("team", "obs"), axis=0, tiled=True)
    factor_cols = jnp.dot(
        inverse_whole,
        jnp.concatenate([block_whole, block_whole], axis=0),
        preferred_element_type=jnp.float32,
    )
    factor_part = lax.dynamic_slice_in_dim(factor_cols, place_index * slab_rows, slab_rows, 0)
    factor_cols = factor_cols.astype(jnp.bfloat16)
    tile_rows = front.shape[0]
    tile_ratio = factor_cols.shape[1] // tile_rows
    offset = place_index % tile_ratio * tile_rows
    own_slice = lax.dynamic_slice_in_dim(factor_cols, offset, tile_rows, 1)
    kept = jnp.where(lax.axis_index("grid") == place_index // tile_ratio, own_slice, 0)
    factor_rows = lax.psum(kept.astype(jnp.bfloat16), "grid")
    return (factor_part, front - contract_rows(factor_rows, factor_cols))


MESH = pl.DeviceIdType.MESH


def column_pieces(cols, tile_rows):
    pieces = []
    for start in range(0, cols, tile_rows):
        wide = tile_rows * 2 // 3
        pieces += [(start, wide), (start + wide, tile_rows - wide)]
    return pieces


def exchange(
    pieces, panel, front_cols, ids, arc_weight, counts, inverse_rows,
    blk, tile, inv_diag, inv_off,
    panels, scaled, weights, outgoing, from_outer, from_inner, own,
    front_sem, panel_send, panel_recv, outer_send, outer_recv, inner_send, inner_recv,
    total_send, total_recv, team_send, team_recv, tile_send, relay_send, tile_recv,
    inv_line_send, inv_line_recv, inv_grid_send, inv_grid_recv, inv_team_send, inv_team_recv,
):
    team, z, grid = lax.axis_index("team"), lax.axis_index("obs"), lax.axis_index("grid")
    rows, width = panel.shape
    lines = inv_diag.shape[1]
    share = inv_diag.shape[3]
    side = inv_off.shape[3]
    x, y = lax.rem(grid, 2), lax.div(grid, 2)
    beside_x = y * 2 + (1 - x)
    beside_y = (1 - y) * 2 + x
    across = (1 - y) * 2 + (1 - x)
    partner = 1 - team
    is_inner = (z == 1) | (z == 2)
    is_outer = jnp.logical_not(is_inner)
    mate = jnp.where(z < 2, 1 - z, 5 - z)
    other = jnp.clip(3 - z, 1, 2)
    half = lax.rem(z, 2)
    root_x = lax.div(z, 2)
    owner = y
    sends_tile = x == root_x
    root_y = team
    is_root = (x == root_x) & (y == root_y)
    at_x = (x != root_x) & (y == root_y)
    at_y = (x == root_x) & (y != root_y)
    at_across = (x != root_x) & (y != root_y)

    barrier = pltpu.get_barrier_semaphore()
    for where in (
        {"grid": beside_x}, {"grid": beside_y}, {"team": partner}, {"obs": mate},
        {"team": partner, "grid": beside_x}, {"team": partner, "grid": beside_y},
    ):
        pl.semaphore_signal(barrier, inc=1, device_id=where, device_id_type=MESH)

    @pl.when(is_inner)
    def _():
        pl.semaphore_signal(barrier, inc=1, device_id={"obs": other}, device_id_type=MESH)

    def load_front(c):
        start, wide = pieces[c]
        at = (slice(None), pl.ds(start, wide))
        return pltpu.make_async_copy(front_cols.at[at], scaled.at[at], front_sem.at[c])

    for c in range(len(pieces)):
        load_front(c).start()

    step = rows // 8
    mine = inverse_rows[pl.ds(pl.multiple_of(grid * share, share), share), :]
    high = mine.astype(jnp.bfloat16)
    row_at = lax.broadcasted_iota(jnp.int32, mine.shape, 0) + (team * side + z * width + grid * share)
    on_diagonal = lax.broadcasted_iota(jnp.int32, mine.shape, 1) == row_at
    rest = jnp.sum(jnp.where(on_diagonal, mine - high.astype(jnp.float32), 0.0), axis=1, keepdims=True)
    rest = jnp.broadcast_to(rest, (share, inv_diag.shape[4] - side)).astype(jnp.bfloat16)

    @pl.when(team == 0)
    def _():
        inv_diag[0, z, grid, :, :side] = high[:, :side]

    @pl.when(team == 1)
    def _():
        inv_diag[1, z, grid, :, :side] = high[:, side:]
        inv_off[z, grid] = high[:, :side]

    inv_diag[team, z, grid, :, side:] = rest

    pl.semaphore_wait(barrier, jnp.where(is_inner, 7, 6))

    def remote(src, dst, send, recv, where):
        return pltpu.make_async_remote_copy(
            src_ref=src, dst_ref=dst, send_sem=send, recv_sem=recv,
            device_id=where, device_id_type=MESH,
        )

    def await_on(ref, sem):
        pltpu.make_async_copy(ref, ref, sem).wait()

    panel_copies = [
        remote(panel, panels.at[0], panel_send.at[0], panel_recv.at[0], {"grid": beside_x}),
        remote(panel, panels.at[1], panel_send.at[1], panel_recv.at[1], {"grid": beside_y}),
    ]
    for copy in panel_copies:
        copy.start()
    top, bottom = pl.ds(0, rows // 2), pl.ds(rows // 2, rows // 2)
    panel_copies += [
        remote(panels.at[0, top], panels.at[2, top], panel_send.at[2], panel_recv.at[2], {"grid": beside_y}),
        remote(panels.at[1, bottom], panels.at[2, bottom], panel_send.at[3], panel_recv.at[3], {"grid": beside_x}),
    ]

    inv_parts = (
        (0, team == 0, lambda *at: inv_diag.at[(0,) + at]),
        (1, team == 1, lambda *at: inv_diag.at[(1,) + at]),
        (2, team == 1, lambda *at: inv_off.at[at]),
    )

    def inv_line(s, what):
        for k, has, of in inv_parts:
            for d, hop in ((0, 1), (1, -1)):
                held = z - hop * s
                sends = (held >= 0) & (held < lines) & (z + hop >= 0) & (z + hop < lines)
                came = z - hop * (s + 1)
                comes = (came >= 0) & (came < lines)
                if what == "start":
                    @pl.when(has & sends)
                    def _():
                        ref = of(jnp.clip(held, 0, lines - 1), grid)
                        remote(ref, ref, inv_line_send.at[k, d, s], inv_line_recv.at[k, d, s],
                               {"obs": jnp.clip(z + hop, 0, lines - 1)}).start()
                elif what == "wait":
                    @pl.when(has & comes)
                    def _():
                        await_on(of(jnp.clip(came, 0, lines - 1), grid), inv_line_recv.at[k, d, s])
                else:
                    @pl.when(has & sends)
                    def _():
                        await_on(of(jnp.clip(held, 0, lines - 1), grid), inv_line_send.at[k, d, s])

    def inv_grid(stage, what):
        every, first, last = pl.ds(0, lines), pl.ds(0, lines // 2), pl.ds(lines // 2, lines // 2)
        for k, has, of in inv_parts:
            moves = (
                (0, (every, grid), (every, beside_x), {"grid": beside_x}),
                (1, (every, grid), (every, beside_y), {"grid": beside_y}),
            ) if stage == 0 else (
                (2, (first, beside_x), (first, across), {"grid": beside_y}),
                (3, (last, beside_y), (last, across), {"grid": beside_x}),
            )

            @pl.when(has)
            def _():
                for j, sent, came, where in moves:
                    if what == "start":
                        remote(of(*sent), of(*sent), inv_grid_send.at[k, j], inv_grid_recv.at[k, j], where).start()
                    elif what == "wait":
                        await_on(of(*came), inv_grid_recv.at[k, j])
                    else:
                        await_on(of(*sent), inv_grid_send.at[k, j])

    def inv_team(what):
        for k, has, of in inv_parts:
            @pl.when(has)
            def _():
                if what == "start":
                    remote(of(), of(), inv_team_send.at[k], inv_team_recv.at[k], {"team": partner}).start()
                elif what == "drain":
                    await_on(of(), inv_team_send.at[k])

            if what == "wait":
                @pl.when(jnp.logical_not(has))
                def _():
                    await_on(of(), inv_team_recv.at[k])

    inv_line(0, "start")

    arcs = arc_weight.shape[1]
    live = counts[0]

    @pl.loop(0, rows // step)
    def _(i):
        at = pl.ds(pl.multiple_of(i * step, step), step)
        hit = ids[at, :] == lax.broadcasted_iota(jnp.int32, (step, arcs), 1)
        looked = jnp.sum(jnp.where(hit, arc_weight[...], 0.0), axis=1, keepdims=True)
        slot = lax.broadcasted_iota(jnp.int32, (step, 1), 0) + i * step
        weights[at, :] = jnp.where(slot < live, looked, 0.0)

    def scale(c):
        start, wide = pieces[c]
        load_front(c).wait()

        @pl.loop(0, rows // step)
        def _(i):
            at = pl.ds(pl.multiple_of(i * step, step), step)
            part = scaled[at, start:start + wide].astype(jnp.float32)
            scaled[at, start:start + wide] = (part * weights[at, :]).astype(jnp.bfloat16)

    count = len(pieces)
    units = [(0, c) for c in range(count)]
    units += [(r, c) for c in range(count // 2) for r in (1, 2)]
    units += [(3, c) for c in range(count // 2)]
    units += [(r, c) for c in range(count // 2, count) for r in (1, 2, 3)]
    source = (grid, beside_x, beside_y, across)

    def piece_at(c):
        return pl.ds(pieces[c][0], pieces[c][1])

    def staged(r, c):
        return pl.ds(r * width, width), piece_at(c)

    def block_rows(t, g):
        return pl.ds(pl.multiple_of((t * 4 + g) * width, width), width)

    def place(t, r, c):
        return block_rows(t, source[r]), piece_at(c)

    def tile_place(t, g, c):
        return block_rows(t, g), pl.ds(pieces[c % (count // 2)][0], pieces[c][1])

    def slot_of(r, c):
        return r * (count // 2) + c % (count // 2)

    def compute(u):
        r, c = units[u]
        if r == 0:
            scale(c)
        start, wide = pieces[c]
        left = panel[...] if r == 0 else panels[r - 1]
        total = contract_rows(left, scaled[:, start:start + wide])
        at = staged(r, c)

        @pl.when(is_inner)
        def _():
            own[at] = total

        @pl.when(is_outer)
        def _():
            outgoing[at] = total.astype(jnp.bfloat16)
            remote(outgoing.at[at], from_outer.at[at], outer_send.at[u], outer_recv.at[u], {"obs": mate}).start()

    def middle(u):
        at = staged(*units[u])
        await_on(from_outer.at[at], outer_recv.at[u])
        total = own[at] + from_outer[at].astype(jnp.float32)
        own[at] = total
        outgoing[at] = total.astype(jnp.bfloat16)
        remote(outgoing.at[at], from_inner.at[at], inner_send.at[u], inner_recv.at[u], {"obs": other}).start()

    def spread(u):
        r, c = units[u]
        ref = blk.at[place(team, r, c)]
        remote(ref, ref, team_send.at[u], team_recv.at[u], {"team": partner}).start()

        @pl.when(sends_tile & (half == c // (count // 2)))
        def _():
            k = slot_of(r, c)
            to = tile.at[tile_place(team, source[r], c)]
            remote(ref, to, tile_send.at[0, k], tile_recv.at[team, k], {"team": owner, "grid": beside_x}).start()
            remote(ref, to, tile_send.at[1, k], tile_recv.at[team, k], {"team": owner, "grid": beside_y}).start()

            @pl.when(team == owner)
            def _():
                pltpu.make_async_copy(ref, to, tile_recv.at[team, k]).start()

            @pl.when(team != owner)
            def _():
                remote(ref, to, tile_send.at[2, k], tile_recv.at[team, k], {"team": partner}).start()

    def finished_inner(u):
        r, c = units[u]
        at = staged(r, c)
        await_on(from_inner.at[at], inner_recv.at[u])
        total = own[at] + from_inner[at].astype(jnp.float32)
        spot = place(team, r, c)
        blk[spot] = total.astype(jnp.bfloat16)
        ref = blk.at[spot]
        remote(ref, ref, total_send.at[u], total_recv.at[u], {"obs": mate}).start()

    def finished_outer(u):
        r, c = units[u]
        await_on(blk.at[place(team, r, c)], total_recv.at[u])

    def tile_source(r):
        root = root_y * 2 + root_x
        flip_x = root_y * 2 + (1 - root_x)
        flip_y = (1 - root_y) * 2 + root_x
        both = (1 - root_y) * 2 + (1 - root_x)
        return (root, flip_x, flip_y, both)[r]

    def relay(u):
        r, c = units[u]
        k = slot_of(r, c)
        even = (r + c) % 2 == 0

        @pl.when((at_x if even else at_y) & (half == c // (count // 2)))
        def _():
            for t in (0, 1):
                ref = tile.at[tile_place(t, tile_source(r), c)]
                await_on(ref, tile_recv.at[t, k])
                remote(ref, ref, relay_send.at[t, k], tile_recv.at[t, k],
                       {"grid": beside_y if even else beside_x}).start()

    last = len(units)
    for i in range(last + 9):
        if i == 1:
            inv_line(0, "wait")
            inv_line(1, "start")
        if i == 2:
            inv_line(1, "wait")
            inv_line(2, "start")
        if i == 3:
            inv_line(2, "wait")
            inv_grid(0, "start")
        if i == count:
            panel_copies[0].wait_recv()
            panel_copies[2].start()
            panel_copies[1].wait_recv()
            panel_copies[3].start()
        if i == count + 2:
            inv_grid(0, "wait")
            inv_grid(1, "start")
        if i == count + count:
            panel_copies[2].wait_recv()
            panel_copies[3].wait_recv()
        if i == count + count + 2:
            inv_grid(1, "wait")
            inv_team("start")

        @pl.when(is_inner)
        def _():
            if 0 <= i - 1 < last:
                middle(i - 1)
            if 0 <= i - 3 < last:
                finished_inner(i - 3)
                spread(i - 3)

        if i < last:
            compute(i)

        @pl.when(is_outer)
        def _():
            if 0 <= i - 5 < last:
                finished_outer(i - 5)
                spread(i - 5)

        @pl.when(is_inner)
        def _():
            if 0 <= i - 5 < last:
                relay(i - 5)

        @pl.when(is_outer)
        def _():
            if 0 <= i - 8 < last:
                relay(i - 8)

    inv_team("wait")
    for u in range(last):
        r, c = units[u]
        k = slot_of(r, c)
        in_half = half == c // (count // 2)
        even = (r + c) % 2 == 0
        await_on(blk.at[place(partner, r, c)], team_recv.at[u])

        @pl.when(in_half & jnp.logical_not(at_x if even else at_y))
        def _():
            for t in (0, 1):
                await_on(tile.at[tile_place(t, tile_source(r), c)], tile_recv.at[t, k])

    for copy in panel_copies:
        copy.wait_send()
    for s in range(lines - 1):
        inv_line(s, "drain")
    inv_grid(0, "drain")
    inv_grid(1, "drain")
    inv_team("drain")
    for u in range(last):
        r, c = units[u]
        k = slot_of(r, c)
        at = staged(r, c)
        in_half = half == c // (count // 2)
        even = (r + c) % 2 == 0
        ref = blk.at[place(team, r, c)]
        await_on(ref, team_send.at[u])

        @pl.when(is_outer)
        def _():
            await_on(outgoing.at[at], outer_send.at[u])

        @pl.when(is_inner)
        def _():
            await_on(outgoing.at[at], inner_send.at[u])
            await_on(ref, total_send.at[u])

        @pl.when(in_half & sends_tile)
        def _():
            await_on(ref, tile_send.at[0, k])
            await_on(ref, tile_send.at[1, k])

            @pl.when(team != owner)
            def _():
                await_on(ref, tile_send.at[2, k])

        @pl.when(in_half & (at_x if even else at_y))
        def _():
            for t in (0, 1):
                await_on(tile.at[tile_place(t, tile_source(r), c)], relay_send.at[t, k])


def finish(blk, tile, inv_diag, inv_off, front, factor_out, front_out, cols, high, low, held, sems):
    team, z = lax.axis_index("team"), lax.axis_index("obs")
    slab, piece = factor_out.shape[0], 2 * factor_out.shape[0]
    side = inv_off.shape[0]
    whole, columns = blk.shape
    tile_cols = tile.shape[1]
    size = 2 * slab
    place = team * (side // slab) + z

    load = pltpu.make_async_copy(front, held, sems.at[0])
    load.start()

    def factor_of(source, at, r):
        rows = slice(r * size, (r + 1) * size)
        t, inner = r * size // side, r * size % side
        near = slice(inner, inner + size)
        total = inv_diag[t, near, side:side + 1].astype(jnp.float32) * source[rows, at].astype(jnp.float32)
        total += jnp.dot(
            inv_diag[t, near, :inner + size], source[t * side:t * side + inner + size, at],
            preferred_element_type=jnp.float32,
        )
        if t:
            total += jnp.dot(inv_off[near, :], source[:side, at], preferred_element_type=jnp.float32)
        return total

    for r in range(whole // size):
        rows = slice(r * size, (r + 1) * size)
        for start in range(0, columns, piece):
            at = slice(start, start + piece)
            value = factor_of(blk, at, r)
            cols[rows, at] = value.astype(jnp.bfloat16)
            for part in range(size // slab):
                @pl.when(place == r * (size // slab) + part)
                def _():
                    factor_out[:, at] = value[part * slab:(part + 1) * slab]
        for start in range(0, tile_cols, piece):
            at = slice(start, start + piece)
            value = factor_of(tile, at, r).T
            upper = value.astype(jnp.bfloat16)
            high[at, rows] = upper
            low[at, rows] = (value - upper.astype(jnp.float32)).astype(jnp.bfloat16)

    load.wait()
    stores = []
    for top in range(0, tile_cols, piece):
        for start in range(0, columns, 2 * piece):
            near, at = slice(top, top + piece), slice(start, start + 2 * piece)
            update = jnp.dot(high[near, :], cols[:, at], preferred_element_type=jnp.float32)
            update += jnp.dot(low[near, :], cols[:, at], preferred_element_type=jnp.float32)
            held[near, at] = held[near, at] - update
            spot = (pl.ds(top, piece), pl.ds(start, 2 * piece))
            stores.append(
                pltpu.make_async_copy(held.at[spot], front_out.at[spot], sems.at[1 + len(stores)])
            )
            stores[-1].start()
    for store in stores:
        store.wait()


def local_kernels(lines, grids, design_panel, design_front, arc_ids, arc_weight, row_counts, panel_inverse, front):
    bf16 = jnp.bfloat16
    slab, whole = panel_inverse.shape
    rows, width = design_panel.shape
    cols = design_front.shape[1]
    tile_rows = front.shape[0]
    side = whole // 2
    share = slab // grids
    pieces = column_pieces(cols, tile_rows)
    vmem = pl.BlockSpec(memory_space=pltpu.VMEM)
    smem = pl.BlockSpec(memory_space=pltpu.SMEM)
    hbm = pl.BlockSpec(memory_space=pl.ANY)
    dma = pltpu.SemaphoreType.DMA
    hops = lines - 1
    units = grids * len(pieces)
    slots = units // 2
    blk, tile, inv_diag, inv_off = pl.pallas_call(
        functools.partial(exchange, pieces),
        out_shape=(
            jax.ShapeDtypeStruct((whole, cols), bf16),
            jax.ShapeDtypeStruct((whole, tile_rows), bf16),
            jax.ShapeDtypeStruct((2, lines, grids, share, side + 128), bf16),
            jax.ShapeDtypeStruct((lines, grids, share, side), bf16),
        ),
        in_specs=[vmem, hbm, vmem, vmem, smem, vmem],
        out_specs=(vmem,) * 4,
        scratch_shapes=[
            pltpu.VMEM((grids - 1, rows, width), bf16),
            pltpu.VMEM((rows, cols), bf16),
            pltpu.VMEM((rows, 1), jnp.float32),
            pltpu.VMEM((grids * width, cols), bf16),
            pltpu.VMEM((grids * width, cols), bf16),
            pltpu.VMEM((grids * width, cols), bf16),
            pltpu.VMEM((grids * width, cols), jnp.float32),
            dma((len(pieces),)), dma((4,)), dma((4,)),
            dma((units,)), dma((units,)), dma((units,)), dma((units,)),
            dma((units,)), dma((units,)), dma((units,)), dma((units,)),
            dma((3, slots)), dma((2, slots)), dma((2, slots)),
            dma((3, 2, hops)), dma((3, 2, hops)), dma((3, 4)), dma((3, 4)), dma((3,)), dma((3,)),
        ],
        compiler_params=pltpu.CompilerParams(
            collective_id=0, has_side_effects=True, vmem_limit_bytes=48 * 2**20
        ),
        name="exchange",
    )(design_panel, design_front, arc_ids[:, None], arc_weight[None, :], row_counts, panel_inverse)
    inv_diag = inv_diag.reshape((2, side, side + 128))
    inv_off = inv_off.reshape((side, side))
    return pl.pallas_call(
        finish,
        out_shape=(
            jax.ShapeDtypeStruct((slab, cols), jnp.float32),
            jax.ShapeDtypeStruct(front.shape, jnp.float32),
        ),
        in_specs=[vmem] * 4 + [hbm],
        out_specs=(vmem, hbm),
        scratch_shapes=[
            pltpu.VMEM((whole, cols), bf16),
            pltpu.VMEM((tile_rows, whole), bf16),
            pltpu.VMEM((tile_rows, whole), bf16),
            pltpu.VMEM(front.shape, jnp.float32),
            dma((1 + tile_rows * cols // (8 * slab * slab),)),
        ],
        compiler_params=pltpu.CompilerParams(vmem_limit_bytes=48 * 2**20),
        name="finish",
    )(blk, tile, inv_diag, inv_off, front)


def solution(mesh):
    placed = (
        P("obs", ("team", "grid")),
        P("obs", "grid"),
        P("obs"),
        P(),
        P("obs"),
        P(("team", "obs"), None),
        P(("team", "obs"), "grid"),
    )
    sizes = mesh.shape
    fits = sizes["team"] == 2 and sizes["obs"] == 4 and sizes["grid"] == 4
    return jax.shard_map(
        functools.partial(local_kernels, sizes["obs"], sizes["grid"]) if fits else local,
        mesh=mesh,
        in_specs=placed,
        out_specs=(P(("team", "obs"), "grid"), P(("team", "obs"), "grid")),
        check_vma=False,
    )
```

```python
import functools

import jax
import jax.numpy as jnp
from jax import lax
from jax.experimental import pallas as pl
from jax.experimental.pallas import tpu as pltpu
from jax.sharding import PartitionSpec as P


def live_weights(arc_ids, arc_weight, row_counts):
    row_total = arc_ids.shape[0]
    arc_total = arc_weight.shape[0]
    hit = arc_ids[:, None] == lax.broadcasted_iota(jnp.int32, (row_total, arc_total), 1)
    looked = jnp.sum(jnp.where(hit, arc_weight[None, :], 0.0), axis=1)
    is_live = lax.broadcasted_iota(jnp.int32, (row_total,), 0) < row_counts[0]
    return looked * is_live.astype(jnp.float32)


def contract_rows(left, right):
    return lax.dot_general(
        left, right, (((0,), (0,)), ((), ())), preferred_element_type=jnp.float32
    )


def local(design_panel, design_front, arc_ids, arc_weight, row_counts, panel_inverse, front):
    high = lax.reduce_precision(panel_inverse, 8, 7)
    split = jnp.concatenate([high, panel_inverse - high], axis=1).astype(jnp.bfloat16)
    inverse_whole = lax.all_gather(split, ("team", "obs"), axis=0, tiled=True)
    weights = live_weights(arc_ids, arc_weight, row_counts)
    scaled_front = (design_front.astype(jnp.float32) * weights[:, None]).astype(jnp.bfloat16)
    panel_piece = lax.all_gather(design_panel, "grid", axis=1, tiled=True)
    partial_value = contract_rows(panel_piece, scaled_front)
    slab_rows = panel_inverse.shape[0]
    place_index = lax.axis_index(("team", "obs"))
    block_part = lax.psum_scatter(partial_value, "obs", scatter_dimension=0, tiled=True)
    block_part = block_part.astype(jnp.bfloat16)
    block_whole = lax.all_gather(block_part, ("team", "obs"), axis=0, tiled=True)
    factor_cols = jnp.dot(
        inverse_whole,
        jnp.concatenate([block_whole, block_whole], axis=0),
        preferred_element_type=jnp.float32,
    )
    factor_part = lax.dynamic_slice_in_dim(factor_cols, place_index * slab_rows, slab_rows, 0)
    factor_cols = factor_cols.astype(jnp.bfloat16)
    tile_rows = front.shape[0]
    tile_ratio = factor_cols.shape[1] // tile_rows
    offset = place_index % tile_ratio * tile_rows
    own_slice = lax.dynamic_slice_in_dim(factor_cols, offset, tile_rows, 1)
    kept = jnp.where(lax.axis_index("grid") == place_index // tile_ratio, own_slice, 0)
    factor_rows = lax.psum(kept.astype(jnp.bfloat16), "grid")
    return (factor_part, front - contract_rows(factor_rows, factor_cols))


MESH = pl.DeviceIdType.MESH


def column_pieces(cols, tile_rows):
    pieces = []
    for start in range(0, cols, tile_rows):
        wide = tile_rows * 2 // 3
        pieces += [(start, wide), (start + wide, tile_rows - wide)]
    return pieces


def exchange(
    pieces, panel, front_cols, ids_hbm, arc_hbm, counts, inverse_hbm, front,
    cols, high, low, held, factor_part,
    blk, tile, inv_diag, inv_off, ids, arc_weight, inverse_rows,
    panels, scaled, weights, outgoing, from_outer, from_inner, own,
    front_sem, local_sem, panel_send, panel_recv, outer_send, outer_recv, inner_send, inner_recv,
    total_send, total_recv, team_send, team_recv, tile_send, relay_send, tile_recv,
    inv_line_send, inv_line_recv, inv_grid_send, inv_grid_recv, inv_team_send, inv_team_recv,
):
    team, z, grid = lax.axis_index("team"), lax.axis_index("obs"), lax.axis_index("grid")
    rows, width = panel.shape
    lines = inv_diag.shape[1]
    share = inv_diag.shape[3]
    side = inv_off.shape[3]
    x, y = lax.rem(grid, 2), lax.div(grid, 2)
    beside_x = y * 2 + (1 - x)
    beside_y = (1 - y) * 2 + x
    across = (1 - y) * 2 + (1 - x)
    partner = 1 - team
    is_inner = (z == 1) | (z == 2)
    is_outer = jnp.logical_not(is_inner)
    mate = jnp.where(z < 2, 1 - z, 5 - z)
    other = jnp.clip(3 - z, 1, 2)
    half = lax.rem(z, 2)
    root_x = lax.div(z, 2)
    owner = y
    sends_tile = x == root_x
    root_y = team
    is_root = (x == root_x) & (y == root_y)
    at_x = (x != root_x) & (y == root_y)
    at_y = (x == root_x) & (y != root_y)
    at_across = (x != root_x) & (y != root_y)

    barrier = pltpu.get_barrier_semaphore()
    for where in (
        {"grid": beside_x}, {"grid": beside_y}, {"team": partner}, {"obs": mate},
        {"team": partner, "grid": beside_x}, {"team": partner, "grid": beside_y},
    ):
        pl.semaphore_signal(barrier, inc=1, device_id=where, device_id_type=MESH)

    @pl.when(is_inner)
    def _():
        pl.semaphore_signal(barrier, inc=1, device_id={"obs": other}, device_id_type=MESH)

    def load_front(c):
        start, wide = pieces[c]
        at = (slice(None), pl.ds(start, wide))
        return pltpu.make_async_copy(front_cols.at[at], scaled.at[at], front_sem.at[c])

    count = len(pieces)
    load_inverse = pltpu.make_async_copy(inverse_hbm, inverse_rows, local_sem.at[0])
    load_ids = pltpu.make_async_copy(ids_hbm, ids, local_sem.at[1])
    load_arcs = pltpu.make_async_copy(arc_hbm, arc_weight, local_sem.at[2])
    load_panel = pltpu.make_async_copy(panel, panels.at[0], local_sem.at[3])
    load_held = pltpu.make_async_copy(front, held, local_sem.at[4])
    load_inverse.start()
    load_ids.start()
    load_arcs.start()
    load_front(0).start()
    load_panel.start()
    for c in range(count // 2, count):
        load_front(c).start()
    for c in range(1, count // 2):
        load_front(c).start()
    load_held.start()

    step = rows // 8
    load_inverse.wait()
    mine = inverse_rows[pl.ds(pl.multiple_of(grid * share, share), share), :]
    rounded = mine.astype(jnp.bfloat16)
    row_at = lax.broadcasted_iota(jnp.int32, mine.shape, 0) + (team * side + z * width + grid * share)
    on_diagonal = lax.broadcasted_iota(jnp.int32, mine.shape, 1) == row_at
    rest = jnp.sum(jnp.where(on_diagonal, mine - rounded.astype(jnp.float32), 0.0), axis=1, keepdims=True)
    rest = jnp.broadcast_to(rest, (share, inv_diag.shape[4] - side)).astype(jnp.bfloat16)

    @pl.when(team == 0)
    def _():
        inv_diag[0, z, grid, :, :side] = rounded[:, :side]

    @pl.when(team == 1)
    def _():
        inv_diag[1, z, grid, :, :side] = rounded[:, side:]
        inv_off[z, grid] = rounded[:, :side]

    inv_diag[team, z, grid, :, side:] = rest

    pl.semaphore_wait(barrier, jnp.where(is_inner, 7, 6))

    def remote(src, dst, send, recv, where):
        return pltpu.make_async_remote_copy(
            src_ref=src, dst_ref=dst, send_sem=send, recv_sem=recv,
            device_id=where, device_id_type=MESH,
        )

    def await_on(ref, sem):
        pltpu.make_async_copy(ref, ref, sem).wait()

    panel_copies = [
        remote(panel, panels.at[1], panel_send.at[0], panel_recv.at[0], {"grid": beside_x}),
        remote(panel, panels.at[2], panel_send.at[1], panel_recv.at[1], {"grid": beside_y}),
    ]
    for copy in panel_copies:
        copy.start()
    top, bottom = pl.ds(0, rows // 2), pl.ds(rows // 2, rows // 2)
    panel_copies += [
        remote(panels.at[1, top], panels.at[3, top], panel_send.at[2], panel_recv.at[2], {"grid": beside_y}),
        remote(panels.at[2, bottom], panels.at[3, bottom], panel_send.at[3], panel_recv.at[3], {"grid": beside_x}),
    ]

    inv_parts = (
        (0, team == 0, lambda *at: inv_diag.at[(0,) + at]),
        (1, team == 1, lambda *at: inv_diag.at[(1,) + at]),
        (2, team == 1, lambda *at: inv_off.at[at]),
    )

    def inv_line(s, what):
        for k, has, of in inv_parts:
            for d, hop in ((0, 1), (1, -1)):
                held = z - hop * s
                sends = (held >= 0) & (held < lines) & (z + hop >= 0) & (z + hop < lines)
                came = z - hop * (s + 1)
                comes = (came >= 0) & (came < lines)
                if what == "start":
                    @pl.when(has & sends)
                    def _():
                        ref = of(jnp.clip(held, 0, lines - 1), grid)
                        remote(ref, ref, inv_line_send.at[k, d, s], inv_line_recv.at[k, d, s],
                               {"obs": jnp.clip(z + hop, 0, lines - 1)}).start()
                elif what == "wait":
                    @pl.when(has & comes)
                    def _():
                        await_on(of(jnp.clip(came, 0, lines - 1), grid), inv_line_recv.at[k, d, s])
                else:
                    @pl.when(has & sends)
                    def _():
                        await_on(of(jnp.clip(held, 0, lines - 1), grid), inv_line_send.at[k, d, s])

    def inv_grid(stage, what):
        every, first, last = pl.ds(0, lines), pl.ds(0, lines // 2), pl.ds(lines // 2, lines // 2)
        for k, has, of in inv_parts:
            moves = (
                (0, (every, grid), (every, beside_x), {"grid": beside_x}),
                (1, (every, grid), (every, beside_y), {"grid": beside_y}),
            ) if stage == 0 else (
                (2, (first, beside_x), (first, across), {"grid": beside_y}),
                (3, (last, beside_y), (last, across), {"grid": beside_x}),
            )

            @pl.when(has)
            def _():
                for j, sent, came, where in moves:
                    if what == "start":
                        remote(of(*sent), of(*sent), inv_grid_send.at[k, j], inv_grid_recv.at[k, j], where).start()
                    elif what == "wait":
                        await_on(of(*came), inv_grid_recv.at[k, j])
                    else:
                        await_on(of(*sent), inv_grid_send.at[k, j])

    def inv_team(what):
        for k, has, of in inv_parts:
            @pl.when(has)
            def _():
                if what == "start":
                    remote(of(), of(), inv_team_send.at[k], inv_team_recv.at[k], {"team": partner}).start()
                elif what == "drain":
                    await_on(of(), inv_team_send.at[k])

            if what == "wait":
                @pl.when(jnp.logical_not(has))
                def _():
                    await_on(of(), inv_team_recv.at[k])

    inv_line(0, "start")

    arcs = arc_weight.shape[1]
    live = counts[0]
    load_ids.wait()
    load_arcs.wait()
    lane = lax.broadcasted_iota(jnp.int32, (arcs, arcs), 1)
    place_of = lax.broadcasted_iota(jnp.int32, (arcs, arcs), 0)

    def upright(line):
        return jnp.sum(jnp.where(lane == place_of, line, 0), axis=1, keepdims=True)

    arc_column = upright(arc_weight[...])
    for i in range(rows // arcs):
        hit = ids[i:i + 1, :] == place_of
        looked = jnp.sum(jnp.where(hit, arc_column, 0.0), axis=0, keepdims=True)
        slot = lax.broadcasted_iota(jnp.int32, (1, arcs), 1) + i * arcs
        weights[i * arcs:(i + 1) * arcs, :] = upright(jnp.where(slot < live, looked, 0.0))

    def scale(c):
        start, wide = pieces[c]
        load_front(c).wait()

        @pl.loop(0, rows // step)
        def _(i):
            at = pl.ds(pl.multiple_of(i * step, step), step)
            part = scaled[at, start:start + wide].astype(jnp.float32)
            scaled[at, start:start + wide] = (part * weights[at, :]).astype(jnp.bfloat16)

    units = [(0, 0), (0, count // 2)]
    units += [(r, 0) for r in (1, 2, 3)] + [(r, count // 2) for r in (1, 2, 3)]
    units += [(r, c) for k in range(1, count // 2) for c in (k, k + count // 2) for r in (0, 1, 2, 3)]
    source = (grid, beside_x, beside_y, across)

    def piece_at(c):
        return pl.ds(pieces[c][0], pieces[c][1])

    def staged(r, c):
        return pl.ds(r * width, width), piece_at(c)

    def block_rows(t, g):
        return pl.ds(pl.multiple_of((t * 4 + g) * width, width), width)

    def place(t, r, c):
        return block_rows(t, source[r]), piece_at(c)

    def tile_place(t, g, c):
        return block_rows(t, g), pl.ds(pieces[c % (count // 2)][0], pieces[c][1])

    def slot_of(r, c):
        return r * (count // 2) + c % (count // 2)

    def compute(u):
        r, c = units[u]
        if r == 0:
            scale(c)
        start, wide = pieces[c]
        total = contract_rows(panels[r], scaled[:, start:start + wide])
        at = staged(r, c)

        @pl.when(is_inner)
        def _():
            own[at] = total

        @pl.when(is_outer)
        def _():
            outgoing[at] = total.astype(jnp.bfloat16)
            remote(outgoing.at[at], from_outer.at[at], outer_send.at[u], outer_recv.at[u], {"obs": mate}).start()

    def middle(u):
        at = staged(*units[u])
        await_on(from_outer.at[at], outer_recv.at[u])
        total = own[at] + from_outer[at].astype(jnp.float32)
        own[at] = total
        outgoing[at] = total.astype(jnp.bfloat16)
        remote(outgoing.at[at], from_inner.at[at], inner_send.at[u], inner_recv.at[u], {"obs": other}).start()

    def spread(u):
        r, c = units[u]
        ref = blk.at[place(team, r, c)]
        remote(ref, ref, team_send.at[u], team_recv.at[u], {"team": partner}).start()

        @pl.when(sends_tile & (half == c // (count // 2)))
        def _():
            k = slot_of(r, c)
            to = tile.at[tile_place(team, source[r], c)]
            remote(ref, to, tile_send.at[0, k], tile_recv.at[team, k], {"team": owner, "grid": beside_x}).start()
            remote(ref, to, tile_send.at[1, k], tile_recv.at[team, k], {"team": owner, "grid": beside_y}).start()

            @pl.when(team == owner)
            def _():
                pltpu.make_async_copy(ref, to, tile_recv.at[team, k]).start()

            @pl.when(team != owner)
            def _():
                remote(ref, to, tile_send.at[2, k], tile_recv.at[team, k], {"team": partner}).start()

    def finished_inner(u):
        r, c = units[u]
        at = staged(r, c)
        await_on(from_inner.at[at], inner_recv.at[u])
        total = own[at] + from_inner[at].astype(jnp.float32)
        spot = place(team, r, c)
        blk[spot] = total.astype(jnp.bfloat16)
        ref = blk.at[spot]
        remote(ref, ref, total_send.at[u], total_recv.at[u], {"obs": mate}).start()

    def finished_outer(u):
        r, c = units[u]
        await_on(blk.at[place(team, r, c)], total_recv.at[u])

    def tile_source(r):
        root = root_y * 2 + root_x
        flip_x = root_y * 2 + (1 - root_x)
        flip_y = (1 - root_y) * 2 + root_x
        both = (1 - root_y) * 2 + (1 - root_x)
        return (root, flip_x, flip_y, both)[r]

    def relay(u):
        r, c = units[u]
        k = slot_of(r, c)
        even = (r + c) % 2 == 0

        @pl.when((at_x if even else at_y) & (half == c // (count // 2)))
        def _():
            for t in (0, 1):
                ref = tile.at[tile_place(t, tile_source(r), c)]
                await_on(ref, tile_recv.at[t, k])
                remote(ref, ref, relay_send.at[t, k], tile_recv.at[t, k],
                       {"grid": beside_y if even else beside_x}).start()

    whole, columns = blk.shape
    slab = inverse_rows.shape[0]
    size = 2 * slab
    blocks = whole // size
    pair = team * lines + z

    def factor_of(ref, at, r):
        t, inner = r * size // side, r * size % side
        first, near = inner // slab, slice(r * size, (r + 1) * size)
        ahead = inv_diag[t, first:first + 2].reshape((size, inv_diag.shape[4]))
        total = ahead[:, side:side + 1].astype(jnp.float32) * ref[near, at].astype(jnp.float32)
        total += jnp.dot(
            ahead[:, :inner + size], ref[t * side:t * side + inner + size, at],
            preferred_element_type=jnp.float32,
        )
        if t:
            behind = inv_off[first:first + 2].reshape((size, side))
            total += jnp.dot(behind, ref[:side, at], preferred_element_type=jnp.float32)
        return total

    def await_columns(c):
        for u in range(last):
            if units[u][1] == c:
                await_on(blk.at[place(partner, *units[u])], team_recv.at[u])

    def factor_columns(c, r):
        at = slice(pieces[c][0], pieces[c][0] + pieces[c][1])
        value = factor_of(blk, at, r)
        cols[r * size:(r + 1) * size, at] = value.astype(jnp.bfloat16)
        for part in range(size // slab):
            @pl.when(pair == r * (size // slab) + part)
            def _():
                factor_part[:, at] = value[part * slab:(part + 1) * slab]

    def await_tile(c):
        for u in range(last):
            r, d = units[u]
            if d % (count // 2) == c:
                k = slot_of(r, d)
                even = (r + d) % 2 == 0

                @pl.when((half == d // (count // 2)) & jnp.logical_not(at_x if even else at_y))
                def _():
                    for t in (0, 1):
                        await_on(tile.at[tile_place(t, tile_source(r), d)], tile_recv.at[t, k])

    def factor_tile(c, r):
        at = slice(pieces[c][0], pieces[c][0] + pieces[c][1])
        value = factor_of(tile, at, r)
        upper = value.astype(jnp.bfloat16)
        high[r * size:(r + 1) * size, at] = upper
        low[r * size:(r + 1) * size, at] = (value - upper.astype(jnp.float32)).astype(jnp.bfloat16)

    def update(c, part):
        at = slice(pieces[c][0], pieces[c][0] + pieces[c][1])
        near = slice(part * size, (part + 1) * size)
        change = contract_rows(high[:, near], cols[:, at]) + contract_rows(low[:, near], cols[:, at])
        held[near, at] = held[near, at] - change

    last = len(units)
    far = count // 2
    tasks = {
        10: [lambda: inv_team("wait"), lambda: await_columns(0)] + [lambda r=r: factor_columns(0, r) for r in range(blocks - 1)],
        11: [lambda: factor_columns(0, blocks - 1)],
        13: [lambda: await_columns(far)] + [lambda r=r: factor_columns(far, r) for r in range(blocks - 1)],
        14: [lambda: factor_columns(far, blocks - 1)],
        17: [lambda: await_columns(1)] + [lambda r=r: factor_columns(1, r) for r in range(blocks)],
        18: [lambda: await_tile(0)] + [lambda r=r: factor_tile(0, r) for r in range(blocks - 1)],
        19: [lambda: factor_tile(0, blocks - 1), load_held.wait],
        20: [lambda: update(0, 0)],
        21: [lambda: update(0, 1)],
        22: [lambda: update(far, 0)],
        23: [lambda: update(far, 1), lambda: update(1, 0), lambda: update(1, 1)],
        24: [lambda: await_columns(far + 1)] + [lambda r=r: factor_columns(far + 1, r) for r in range(blocks)],
        25: [lambda: await_tile(1)] + [lambda r=r: factor_tile(1, r) for r in range(blocks)],
    }
    for i in range(last + 10):
        if i == 0:
            load_panel.wait()
        if i == 1:
            inv_line(0, "wait")
            inv_line(1, "start")
        if i == 2:
            inv_line(1, "wait")
            inv_line(2, "start")
        if i == 3:
            inv_line(2, "wait")
            inv_grid(0, "start")
        if i == 6:
            inv_grid(0, "wait")
            inv_grid(1, "start")
        if i == 8:
            inv_grid(1, "wait")
            inv_team("start")

        @pl.when(is_inner)
        def _():
            if 0 <= i - 1 < last:
                middle(i - 1)
            if 0 <= i - 3 < last:
                finished_inner(i - 3)
                spread(i - 3)

        if i == 2:
            panel_copies[0].wait_recv()
            panel_copies[2].start()
            panel_copies[1].wait_recv()
            panel_copies[3].start()
        if i == 4:
            panel_copies[2].wait_recv()
            panel_copies[3].wait_recv()

        if i < last:
            compute(i)

        @pl.when(is_outer)
        def _():
            if 0 <= i - 5 < last:
                finished_outer(i - 5)
                spread(i - 5)

        @pl.when(is_inner)
        def _():
            if 0 <= i - 5 < last:
                relay(i - 5)

        @pl.when(is_outer)
        def _():
            if 0 <= i - 7 < last:
                relay(i - 7)

        for task in tasks.get(i, ()):
            task()

    for copy in panel_copies:
        copy.wait_send()
    for s in range(lines - 1):
        inv_line(s, "drain")
    inv_grid(0, "drain")
    inv_grid(1, "drain")
    inv_team("drain")
    for u in range(last):
        r, c = units[u]
        k = slot_of(r, c)
        at = staged(r, c)
        in_half = half == c // (count // 2)
        even = (r + c) % 2 == 0
        ref = blk.at[place(team, r, c)]
        await_on(ref, team_send.at[u])

        @pl.when(is_outer)
        def _():
            await_on(outgoing.at[at], outer_send.at[u])

        @pl.when(is_inner)
        def _():
            await_on(outgoing.at[at], inner_send.at[u])
            await_on(ref, total_send.at[u])

        @pl.when(in_half & sends_tile)
        def _():
            await_on(ref, tile_send.at[0, k])
            await_on(ref, tile_send.at[1, k])

            @pl.when(team != owner)
            def _():
                await_on(ref, tile_send.at[2, k])

        @pl.when(in_half & (at_x if even else at_y))
        def _():
            for t in (0, 1):
                await_on(tile.at[tile_place(t, tile_source(r), c)], relay_send.at[t, k])


def finish(pieces, cols, high, low, held, factor_part, factor_out, front_out, done, sems):
    count = len(pieces)
    tile_rows, columns = held.shape
    wide = pieces[0][1]
    ready = [0, count // 2, 1]
    copies = [pltpu.make_async_copy(factor_part, factor_out, sems.at[0])]

    def store(ref, near, start, width):
        at = (pl.ds(near[0], near[1]), pl.ds(start, width))
        copies.append(pltpu.make_async_copy(ref.at[at], front_out.at[at], sems.at[len(copies)]))
        copies[-1].start()

    copies[0].start()
    for c in ready:
        store(held, (0, wide), *pieces[c])

    def update(near, start, width):
        rows, at = slice(near[0], near[0] + near[1]), slice(start, start + width)
        change = contract_rows(high[:, rows], cols[:, at]) + contract_rows(low[:, rows], cols[:, at])
        done[rows, at] = held[rows, at] - change
        store(done, near, start, width)

    final = pieces[count // 2 + 1]
    update((0, wide), *final)
    for start, width in pieces[0::2] + pieces[1::2]:
        update((wide, tile_rows - wide), start, width)
    for copy in copies:
        copy.wait()


def local_kernels(lines, grids, design_panel, design_front, arc_ids, arc_weight, row_counts, panel_inverse, front):
    bf16 = jnp.bfloat16
    slab, whole = panel_inverse.shape
    rows, width = design_panel.shape
    cols = design_front.shape[1]
    tile_rows = front.shape[0]
    side = whole // 2
    share = slab // grids
    pieces = column_pieces(cols, tile_rows)
    vmem = pl.BlockSpec(memory_space=pltpu.VMEM)
    smem = pl.BlockSpec(memory_space=pltpu.SMEM)
    hbm = pl.BlockSpec(memory_space=pltpu.HBM)
    dma = pltpu.SemaphoreType.DMA
    hops = lines - 1
    arcs = arc_weight.shape[0]

    def stay(value):
        return pltpu.with_memory_space_constraint(value, pltpu.HBM)

    units = grids * len(pieces)
    slots = units // 2
    f32 = jnp.float32
    outs = pl.pallas_call(
        functools.partial(exchange, pieces),
        out_shape=(
            jax.ShapeDtypeStruct((whole, cols), bf16),
            jax.ShapeDtypeStruct((whole, tile_rows), bf16),
            jax.ShapeDtypeStruct((whole, tile_rows), bf16),
            jax.ShapeDtypeStruct(front.shape, f32),
            jax.ShapeDtypeStruct((slab, cols), f32),
        ),
        in_specs=[hbm, hbm, hbm, hbm, smem, hbm, hbm],
        out_specs=(vmem,) * 5,
        scratch_shapes=[
            pltpu.VMEM((whole, cols), bf16),
            pltpu.VMEM((whole, tile_rows), bf16),
            pltpu.VMEM((2, lines, grids, share, side + 128), bf16),
            pltpu.VMEM((lines, grids, share, side), bf16),
            pltpu.VMEM((rows // arcs, arcs), jnp.int32),
            pltpu.VMEM((1, arcs), f32),
            pltpu.VMEM((slab, whole), f32),
            pltpu.VMEM((grids, rows, width), bf16),
            pltpu.VMEM((rows, cols), bf16),
            pltpu.VMEM((rows, 1), f32),
            pltpu.VMEM((grids * width, cols), bf16),
            pltpu.VMEM((grids * width, cols), bf16),
            pltpu.VMEM((grids * width, cols), bf16),
            pltpu.VMEM((grids * width, cols), f32),
            dma((len(pieces),)), dma((5,)), dma((4,)), dma((4,)),
            dma((units,)), dma((units,)), dma((units,)), dma((units,)),
            dma((units,)), dma((units,)), dma((units,)), dma((units,)),
            dma((3, slots)), dma((2, slots)), dma((2, slots)),
            dma((3, 2, hops)), dma((3, 2, hops)), dma((3, 4)), dma((3, 4)), dma((3,)), dma((3,)),
        ],
        compiler_params=pltpu.CompilerParams(
            collective_id=0, has_side_effects=True, vmem_limit_bytes=30 * 2**20
        ),
        name="exchange",
    )(stay(design_panel), stay(design_front), stay(arc_ids.reshape((rows // arcs, arcs))),
      stay(arc_weight[None, :]), row_counts, stay(panel_inverse), stay(front))
    return pl.pallas_call(
        functools.partial(finish, pieces),
        out_shape=(
            jax.ShapeDtypeStruct((slab, cols), f32),
            jax.ShapeDtypeStruct(front.shape, f32),
        ),
        in_specs=[vmem] * 5,
        out_specs=(hbm, hbm),
        scratch_shapes=[
            pltpu.VMEM(front.shape, f32),
            dma((2 * len(pieces) + 1,)),
        ],
        compiler_params=pltpu.CompilerParams(vmem_limit_bytes=12 * 2**20),
        name="finish",
    )(*outs)


def solution(mesh):
    placed = (
        P("obs", ("team", "grid")),
        P("obs", "grid"),
        P("obs"),
        P(),
        P("obs"),
        P(("team", "obs"), None),
        P(("team", "obs"), "grid"),
    )
    sizes = mesh.shape
    fits = sizes["team"] == 2 and sizes["obs"] == 4 and sizes["grid"] == 4
    return jax.shard_map(
        functools.partial(local_kernels, sizes["obs"], sizes["grid"]) if fits else local,
        mesh=mesh,
        in_specs=placed,
        out_specs=(P(("team", "obs"), "grid"), P(("team", "obs"), "grid")),
        check_vma=False,
    )
```

```python
import functools

import jax
import jax.numpy as jnp
from jax import lax
from jax.experimental import pallas as pl
from jax.experimental.pallas import tpu as pltpu
from jax.sharding import PartitionSpec as P


def live_weights(arc_ids, arc_weight, row_counts):
    row_total = arc_ids.shape[0]
    arc_total = arc_weight.shape[0]
    hit = arc_ids[:, None] == lax.broadcasted_iota(jnp.int32, (row_total, arc_total), 1)
    looked = jnp.sum(jnp.where(hit, arc_weight[None, :], 0.0), axis=1)
    is_live = lax.broadcasted_iota(jnp.int32, (row_total,), 0) < row_counts[0]
    return looked * is_live.astype(jnp.float32)


def contract_rows(left, right):
    return lax.dot_general(
        left, right, (((0,), (0,)), ((), ())), preferred_element_type=jnp.float32
    )


def local(design_panel, design_front, arc_ids, arc_weight, row_counts, panel_inverse, front):
    high = lax.reduce_precision(panel_inverse, 8, 7)
    split = jnp.concatenate([high, panel_inverse - high], axis=1).astype(jnp.bfloat16)
    inverse_whole = lax.all_gather(split, ("team", "obs"), axis=0, tiled=True)
    weights = live_weights(arc_ids, arc_weight, row_counts)
    scaled_front = (design_front.astype(jnp.float32) * weights[:, None]).astype(jnp.bfloat16)
    panel_piece = lax.all_gather(design_panel, "grid", axis=1, tiled=True)
    partial_value = contract_rows(panel_piece, scaled_front)
    slab_rows = panel_inverse.shape[0]
    place_index = lax.axis_index(("team", "obs"))
    block_part = lax.psum_scatter(partial_value, "obs", scatter_dimension=0, tiled=True)
    block_part = block_part.astype(jnp.bfloat16)
    block_whole = lax.all_gather(block_part, ("team", "obs"), axis=0, tiled=True)
    factor_cols = jnp.dot(
        inverse_whole,
        jnp.concatenate([block_whole, block_whole], axis=0),
        preferred_element_type=jnp.float32,
    )
    factor_part = lax.dynamic_slice_in_dim(factor_cols, place_index * slab_rows, slab_rows, 0)
    factor_cols = factor_cols.astype(jnp.bfloat16)
    tile_rows = front.shape[0]
    tile_ratio = factor_cols.shape[1] // tile_rows
    offset = place_index % tile_ratio * tile_rows
    own_slice = lax.dynamic_slice_in_dim(factor_cols, offset, tile_rows, 1)
    kept = jnp.where(lax.axis_index("grid") == place_index // tile_ratio, own_slice, 0)
    factor_rows = lax.psum(kept.astype(jnp.bfloat16), "grid")
    return (factor_part, front - contract_rows(factor_rows, factor_cols))


MESH = pl.DeviceIdType.MESH


UNITS = (
    (0, 0), (0, 3), (0, 1), (0, 4), (0, 2), (0, 5), (1, 0), (1, 3), (1, 1), (1, 4), (2, 0), (2, 3), (2, 1),
    (2, 4), (3, 0), (3, 3), (3, 1), (3, 4), (1, 2), (2, 2), (3, 2), (1, 5), (2, 5), (3, 5)
)
INNER = (
    (0, 0, 4), (0, 1, 6), (0, 2, 7), (1, 0, 8), (0, 3, 8), (0, 4, 10), (1, 1, 10), (0, 5, 10), (1, 2, 10), (0,
    6, 10), (1, 3, 11), (0, 7, 12), (1, 4, 12), (0, 8, 14), (1, 5, 14), (0, 9, 14), (1, 6, 14), (0, 10, 14),
    (1, 7, 14), (0, 11, 14), (1, 8, 15), (0, 12, 16), (1, 9, 16), (0, 13, 18), (1, 10, 18), (0, 14, 19), (2,
    0, 19), (1, 11, 19), (2, 1, 19), (0, 15, 21), (1, 12, 21), (2, 2, 21), (2, 3, 21), (0, 16, 22), (1, 13,
    22), (2, 4, 22), (2, 5, 22), (0, 17, 23), (2, 6, 23), (1, 14, 23), (2, 7, 23), (2, 8, 24), (0, 18, 24),
    (1, 15, 24), (2, 9, 24), (0, 19, 28), (1, 16, 28), (2, 10, 28), (2, 11, 28), (0, 20, 31), (1, 17, 31), (2,
    12, 31), (2, 13, 31), (0, 21, 34), (2, 14, 34), (1, 18, 34), (2, 15, 34), (0, 22, 37), (1, 19, 37), (2,
    16, 37), (2, 17, 39), (0, 23, 40), (1, 20, 40), (2, 18, 40), (1, 21, 42), (2, 19, 44), (1, 22, 45), (2,
    20, 46), (1, 23, 47), (2, 21, 47), (2, 22, 52), (2, 23, 55)
)
OUTER = (
    (1, 0, 10), (1, 1, 12), (1, 2, 14), (1, 3, 14), (1, 4, 14), (1, 5, 14), (1, 6, 17), (1, 7, 19), (1, 8,
    21), (2, 0, 21), (2, 1, 21), (1, 9, 23), (2, 2, 23), (2, 3, 23), (2, 4, 24), (1, 10, 24), (2, 5, 24), (2,
    6, 24), (1, 11, 24), (2, 7, 24), (2, 8, 24), (1, 12, 24), (2, 9, 24), (2, 10, 24), (1, 13, 24), (2, 11,
    24), (1, 14, 24), (2, 12, 24), (1, 15, 25), (2, 13, 27), (1, 16, 29), (2, 14, 31), (1, 17, 33), (2, 15,
    35), (1, 18, 37), (2, 16, 39), (1, 19, 40), (2, 17, 40), (1, 20, 42), (2, 18, 44), (1, 21, 45), (2, 19,
    46), (1, 22, 47), (2, 20, 48), (1, 23, 50), (2, 21, 52), (2, 22, 54), (2, 23, 59)
)


def exchange(
    panel, front_cols, ids_hbm, arc_hbm, counts, inverse_hbm, front,
    cols, high, low, held, factor_part,
    blk, tile, inv_diag, inv_off, ids, arc_weight, inverse_rows,
    panels, scaled, weights, outgoing, from_outer, from_inner, own,
    front_sem, local_sem, panel_send, panel_recv, outer_send, outer_recv, inner_send, inner_recv,
    total_send, total_recv, team_send, team_recv, tile_send, relay_send, tile_recv,
    inv_line_send, inv_line_recv, inv_grid_send, inv_grid_recv, inv_team_send, inv_team_recv,
):
    team, z, grid = lax.axis_index("team"), lax.axis_index("obs"), lax.axis_index("grid")
    rows, width = panel.shape
    lines = inv_diag.shape[1]
    share = inv_diag.shape[3]
    side = inv_off.shape[3]
    x, y = lax.rem(grid, 2), lax.div(grid, 2)
    beside_x = y * 2 + (1 - x)
    beside_y = (1 - y) * 2 + x
    across = (1 - y) * 2 + (1 - x)
    partner = 1 - team
    is_inner = (z == 1) | (z == 2)
    is_outer = jnp.logical_not(is_inner)
    mate = jnp.where(z < 2, 1 - z, 5 - z)
    other = jnp.clip(3 - z, 1, 2)
    half = lax.rem(z, 2)
    root_x = lax.div(z, 2)
    owner = y
    sends_tile = x == root_x
    root_y = team
    is_root = (x == root_x) & (y == root_y)
    at_x = (x != root_x) & (y == root_y)
    at_y = (x == root_x) & (y != root_y)
    at_across = (x != root_x) & (y != root_y)

    barrier = pltpu.get_barrier_semaphore()
    for where in (
        {"grid": beside_x}, {"grid": beside_y}, {"team": partner}, {"obs": mate},
        {"team": partner, "grid": beside_x}, {"team": partner, "grid": beside_y},
    ):
        pl.semaphore_signal(barrier, inc=1, device_id=where, device_id_type=MESH)

    @pl.when(is_inner)
    def _():
        pl.semaphore_signal(barrier, inc=1, device_id={"obs": other}, device_id_type=MESH)

    count, side_pieces = blk.shape[0], tile.shape[0]
    wide = blk.shape[2]

    def load_front(c):
        at = (slice(None), pl.ds(c * wide, wide))
        return pltpu.make_async_copy(front_cols.at[at], scaled.at[at], front_sem.at[c])

    load_inverse = pltpu.make_async_copy(inverse_hbm, inverse_rows, local_sem.at[0])
    load_ids = pltpu.make_async_copy(ids_hbm, ids, local_sem.at[1])
    load_arcs = pltpu.make_async_copy(arc_hbm, arc_weight, local_sem.at[2])
    load_panel = pltpu.make_async_copy(panel, panels.at[0], local_sem.at[3])
    load_held = pltpu.make_async_copy(front, held, local_sem.at[4])
    load_inverse.start()
    load_ids.start()
    load_arcs.start()
    load_front(0).start()
    load_panel.start()
    for r, c in UNITS[1:count]:
        load_front(c).start()
    load_held.start()

    step = rows // 8
    load_inverse.wait()
    mine = inverse_rows[pl.ds(pl.multiple_of(grid * share, share), share), :]
    rounded = mine.astype(jnp.bfloat16)
    row_at = lax.broadcasted_iota(jnp.int32, mine.shape, 0) + (team * side + z * width + grid * share)
    on_diagonal = lax.broadcasted_iota(jnp.int32, mine.shape, 1) == row_at
    rest = jnp.sum(jnp.where(on_diagonal, mine - rounded.astype(jnp.float32), 0.0), axis=1, keepdims=True)
    rest = jnp.broadcast_to(rest, (share, inv_diag.shape[4] - side)).astype(jnp.bfloat16)

    @pl.when(team == 0)
    def _():
        inv_diag[0, z, grid, :, :side] = rounded[:, :side]

    @pl.when(team == 1)
    def _():
        inv_diag[1, z, grid, :, :side] = rounded[:, side:]
        inv_off[z, grid] = rounded[:, :side]

    inv_diag[team, z, grid, :, side:] = rest

    pl.semaphore_wait(barrier, jnp.where(is_inner, 7, 6))

    def remote(src, dst, send, recv, where):
        return pltpu.make_async_remote_copy(
            src_ref=src, dst_ref=dst, send_sem=send, recv_sem=recv,
            device_id=where, device_id_type=MESH,
        )

    def await_on(ref, sem):
        pltpu.make_async_copy(ref, ref, sem).wait()

    first = jnp.where(team == 0, beside_x, beside_y)
    second = jnp.where(team == 0, beside_y, beside_x)
    top, bottom = pl.ds(0, rows // 2), pl.ds(rows // 2, rows // 2)
    panel_copies = [
        remote(panel, panels.at[1], panel_send.at[0], panel_recv.at[0], {"grid": first}),
        remote(panel, panels.at[2], panel_send.at[1], panel_recv.at[1], {"grid": second}),
        remote(panels.at[1, top], panels.at[3, top], panel_send.at[2], panel_recv.at[2], {"grid": second}),
        remote(panels.at[2, bottom], panels.at[3, bottom], panel_send.at[3], panel_recv.at[3], {"grid": first}),
    ]
    panel_copies[0].start()

    inv_parts = (
        (0, team == 0, lambda *at: inv_diag.at[(0,) + at]),
        (1, team == 1, lambda *at: inv_diag.at[(1,) + at]),
        (2, team == 1, lambda *at: inv_off.at[at]),
    )

    def inv_line(s, what):
        for k, has, of in inv_parts:
            for d, hop in ((0, 1), (1, -1)):
                held = z - hop * s
                sends = (held >= 0) & (held < lines) & (z + hop >= 0) & (z + hop < lines)
                came = z - hop * (s + 1)
                comes = (came >= 0) & (came < lines)
                if what == "start":
                    @pl.when(has & sends)
                    def _():
                        ref = of(jnp.clip(held, 0, lines - 1), grid)
                        remote(ref, ref, inv_line_send.at[k, d, s], inv_line_recv.at[k, d, s],
                               {"obs": jnp.clip(z + hop, 0, lines - 1)}).start()
                elif what == "wait":
                    @pl.when(has & comes)
                    def _():
                        await_on(of(jnp.clip(came, 0, lines - 1), grid), inv_line_recv.at[k, d, s])
                else:
                    @pl.when(has & sends)
                    def _():
                        await_on(of(jnp.clip(held, 0, lines - 1), grid), inv_line_send.at[k, d, s])

    def inv_grid(stage, what):
        every, first, last = pl.ds(0, lines), pl.ds(0, lines // 2), pl.ds(lines // 2, lines // 2)
        for k, has, of in inv_parts:
            moves = (
                (0, (every, grid), (every, beside_x), {"grid": beside_x}),
                (1, (every, grid), (every, beside_y), {"grid": beside_y}),
            ) if stage == 0 else (
                (2, (first, beside_x), (first, across), {"grid": beside_y}),
                (3, (last, beside_y), (last, across), {"grid": beside_x}),
            )

            @pl.when(has)
            def _():
                for j, sent, came, where in moves:
                    if what == "start":
                        remote(of(*sent), of(*sent), inv_grid_send.at[k, j], inv_grid_recv.at[k, j], where).start()
                    elif what == "wait":
                        await_on(of(*came), inv_grid_recv.at[k, j])
                    else:
                        await_on(of(*sent), inv_grid_send.at[k, j])

    def inv_team(what):
        for k, has, of in inv_parts:
            @pl.when(has)
            def _():
                if what == "start":
                    remote(of(), of(), inv_team_send.at[k], inv_team_recv.at[k], {"team": partner}).start()
                elif what == "drain":
                    await_on(of(), inv_team_send.at[k])

            if what == "wait":
                @pl.when(jnp.logical_not(has))
                def _():
                    await_on(of(), inv_team_recv.at[k])

    inv_line(0, "start")

    arcs = arc_weight.shape[1]
    live = counts[0]
    load_ids.wait()
    load_arcs.wait()
    lane = lax.broadcasted_iota(jnp.int32, (arcs, arcs), 1)
    place_of = lax.broadcasted_iota(jnp.int32, (arcs, arcs), 0)

    def upright(line):
        return jnp.sum(jnp.where(lane == place_of, line, 0), axis=1, keepdims=True)

    arc_column = upright(arc_weight[...])
    for i in range(rows // arcs):
        hit = ids[i:i + 1, :] == place_of
        looked = jnp.sum(jnp.where(hit, arc_column, 0.0), axis=0, keepdims=True)
        slot = lax.broadcasted_iota(jnp.int32, (1, arcs), 1) + i * arcs
        weights[i * arcs:(i + 1) * arcs, :] = upright(jnp.where(slot < live, looked, 0.0))

    def scale(c):
        at_cols = slice(c * wide, (c + 1) * wide)
        load_front(c).wait()

        @pl.loop(0, rows // step)
        def _(i):
            at = pl.ds(pl.multiple_of(i * step, step), step)
            part = scaled[at, at_cols].astype(jnp.float32)
            scaled[at, at_cols] = (part * weights[at, :]).astype(jnp.bfloat16)

    def source(t, r):
        if r == 0:
            return grid
        if r == 3:
            return across
        return jnp.where(t == r - 1, beside_x, beside_y)

    def tile_source(t, r):
        root = root_y * 2 + root_x
        flip_x = root_y * 2 + (1 - root_x)
        flip_y = (1 - root_y) * 2 + root_x
        both = (1 - root_y) * 2 + (1 - root_x)
        return (root, (flip_x, flip_y)[t], (flip_y, flip_x)[t], both)[r]

    def staged(r, c):
        return c, pl.ds(r * width, width)

    def block_rows(t, g):
        return pl.ds(pl.multiple_of((t * 4 + g) * width, width), width)

    def place(t, r, c):
        return c, block_rows(t, source(t, r))

    def tile_place(t, r, c):
        return c % side_pieces, block_rows(t, tile_source(t, r))

    def slot_of(r, c):
        return r * side_pieces + c % side_pieces

    def in_half(c):
        return half == c // side_pieces

    def compute(u):
        r, c = UNITS[u]
        if r == 0:
            scale(c)
        total = contract_rows(panels[r], scaled[:, c * wide:(c + 1) * wide])
        at = staged(r, c)

        @pl.when(is_inner)
        def _():
            own[at] = total

        @pl.when(is_outer)
        def _():
            outgoing[at] = total.astype(jnp.bfloat16)
            remote(outgoing.at[at], from_outer.at[at], outer_send.at[u], outer_recv.at[u], {"obs": mate}).start()

    def middle(u):
        at = staged(*UNITS[u])
        await_on(from_outer.at[at], outer_recv.at[u])
        total = own[at] + from_outer[at].astype(jnp.float32)
        own[at] = total
        outgoing[at] = total.astype(jnp.bfloat16)
        remote(outgoing.at[at], from_inner.at[at], inner_send.at[u], inner_recv.at[u], {"obs": other}).start()

    def spread_tile(u):
        r, c = UNITS[u]
        ref = blk.at[place(team, r, c)]

        @pl.when(sends_tile & in_half(c))
        def _():
            k = slot_of(r, c)
            to = tile.at[c % side_pieces, block_rows(team, source(team, r))]
            remote(ref, to, tile_send.at[0, k], tile_recv.at[team, k], {"team": owner, "grid": beside_x}).start()
            remote(ref, to, tile_send.at[1, k], tile_recv.at[team, k], {"team": owner, "grid": beside_y}).start()

            @pl.when(team == owner)
            def _():
                pltpu.make_async_copy(ref, to, tile_recv.at[team, k]).start()

            @pl.when(team != owner)
            def _():
                remote(ref, to, tile_send.at[2, k], tile_recv.at[team, k], {"team": partner}).start()

    def spread(u):
        ref = blk.at[place(team, *UNITS[u])]
        if u >= count:
            spread_tile(u)
        remote(ref, ref, team_send.at[u], team_recv.at[u], {"team": partner}).start()

    def finished_inner(u):
        r, c = UNITS[u]
        at = staged(r, c)
        await_on(from_inner.at[at], inner_recv.at[u])
        total = own[at] + from_inner[at].astype(jnp.float32)
        spot = place(team, r, c)
        blk[spot] = total.astype(jnp.bfloat16)
        ref = blk.at[spot]
        remote(ref, ref, total_send.at[u], total_recv.at[u], {"obs": mate}).start()
        spread(u)

    def finished_outer(u):
        await_on(blk.at[place(team, *UNITS[u])], total_recv.at[u])
        spread(u)

    def relay(u):
        r, c = UNITS[u]
        k = slot_of(r, c)

        @pl.when(at_x & in_half(c))
        def _():
            for t in (0, 1):
                ref = tile.at[tile_place(t, r, c)]
                await_on(ref, tile_recv.at[t, k])
                remote(ref, ref, relay_send.at[t, k], tile_recv.at[t, k], {"grid": beside_y}).start()

    slab = inverse_rows.shape[0]
    size = 2 * slab
    blocks = blk.shape[1] // size
    pair = team * lines + z

    def factor_of(ref, c, r):
        t, inner = r * size // side, r * size % side
        begin, near = inner // slab, slice(r * size, (r + 1) * size)
        ahead = inv_diag[t, begin:begin + 2].reshape((size, inv_diag.shape[4]))
        total = ahead[:, side:side + 1].astype(jnp.float32) * ref[c, near].astype(jnp.float32)
        total += jnp.dot(
            ahead[:, :inner + size], ref[c, t * side:t * side + inner + size],
            preferred_element_type=jnp.float32,
        )
        if t:
            behind = inv_off[begin:begin + 2].reshape((size, side))
            total += jnp.dot(behind, ref[c, :side], preferred_element_type=jnp.float32)
        return total

    def factor_columns(c, r):
        if r == 0:
            for u in range(len(UNITS)):
                if UNITS[u][1] == c:
                    await_on(blk.at[place(partner, *UNITS[u])], team_recv.at[u])
        value = factor_of(blk, c, r)
        cols[c, r * size:(r + 1) * size] = value.astype(jnp.bfloat16)
        for part in range(size // slab):
            @pl.when(pair == r * (size // slab) + part)
            def _():
                factor_part[:, c * wide:(c + 1) * wide] = value[part * slab:(part + 1) * slab]

    def factor_tile(j, r):
        if r == 0:
            for d, c in UNITS:
                if c % side_pieces == j:
                    @pl.when(in_half(c) & jnp.logical_not(at_x))
                    def _():
                        for t in (0, 1):
                            await_on(tile.at[tile_place(t, d, c)], tile_recv.at[t, slot_of(d, c)])
        value = factor_of(tile, j, r)
        upper = value.astype(jnp.bfloat16)
        high[j, r * size:(r + 1) * size] = upper
        low[j, r * size:(r + 1) * size] = (value - upper.astype(jnp.float32)).astype(jnp.bfloat16)

    def update(c, j):
        near, at = slice(j * wide, (j + 1) * wide), slice(c * wide, (c + 1) * wide)
        change = contract_rows(high[j], cols[c]) + contract_rows(low[j], cols[c])
        held[near, at] = held[near, at] - change

    last = len(UNITS)
    work = [(compute, (u,)) for u in range(last)]

    def columns_work(c):
        return [(factor_columns, (c, r)) for r in range(blocks)]

    def tile_work(j):
        return [(factor_tile, (j, r)) for r in range(blocks)]

    def update_work(cs, js):
        return [(update, (c, j)) for j in js for c in cs]

    work += columns_work(0) + columns_work(3) + columns_work(1) + columns_work(4)
    work += tile_work(0) + update_work((0, 3, 1, 4), (0,))
    work += tile_work(1) + update_work((0, 3), (1,)) + columns_work(2) + update_work((1, 4), (1,))
    work += update_work((2,), (0, 1)) + columns_work(5) + tile_work(2)
    starts = [min(u for u in range(last) if UNITS[u][0] == r) for r in range(4)]

    def hooks(i):
        if i == 0:
            load_panel.wait()
        if i == 2:
            inv_line(0, "wait")
            inv_line(1, "start")
        if i == 4:
            inv_line(1, "wait")
            inv_line(2, "start")
        if i == 5:
            panel_copies[0].wait_send()
            panel_copies[1].start()
        if i == starts[1]:
            inv_line(2, "wait")
            panel_copies[0].wait_recv()
            panel_copies[2].start()
        if i == starts[2]:
            panel_copies[1].wait_recv()
            panel_copies[3].start()
            inv_grid(0, "start")
        if i == starts[3]:
            panel_copies[2].wait_recv()
            panel_copies[3].wait_recv()
        if i == starts[3] + 1:
            for u in range(count):
                spread_tile(u)
        if i == starts[3] + 5:
            inv_grid(0, "wait")
            inv_grid(1, "start")
        if i == starts[3] + 8:
            inv_grid(1, "wait")
            inv_team("start")
        if i == last:
            inv_team("wait")
        if i == last + 5 * blocks:
            load_held.wait()

    def role_work(steps, functions, i):
        for kind, u, at in steps:
            if at == i:
                functions[kind](u)

    for i in range(len(work) + 1):
        if any(at == i for _, _, at in INNER):
            @pl.when(is_inner)
            def _():
                role_work(INNER, (middle, finished_inner, relay), i)

        if any(at == i for _, _, at in OUTER):
            @pl.when(is_outer)
            def _():
                role_work(OUTER, (None, finished_outer, relay), i)

        hooks(i)
        if i < len(work):
            function, at = work[i]
            function(*at)

    for copy in (panel_copies[1], panel_copies[2], panel_copies[3]):
        copy.wait_send()
    for s in range(lines - 1):
        inv_line(s, "drain")
    inv_grid(0, "drain")
    inv_grid(1, "drain")
    inv_team("drain")
    for u in range(last):
        r, c = UNITS[u]
        k = slot_of(r, c)
        at = staged(r, c)
        ref = blk.at[place(team, r, c)]
        await_on(ref, team_send.at[u])

        @pl.when(is_outer)
        def _():
            await_on(outgoing.at[at], outer_send.at[u])

        @pl.when(is_inner)
        def _():
            await_on(outgoing.at[at], inner_send.at[u])
            await_on(ref, total_send.at[u])

        @pl.when(in_half(c) & sends_tile)
        def _():
            await_on(ref, tile_send.at[0, k])
            await_on(ref, tile_send.at[1, k])

            @pl.when(team != owner)
            def _():
                await_on(ref, tile_send.at[2, k])

        @pl.when(in_half(c) & at_x)
        def _():
            for t in (0, 1):
                await_on(tile.at[tile_place(t, r, c)], relay_send.at[t, k])


def finish(cols, high, low, held, factor_part, factor_out, front_out, done, sems):
    count, side_pieces = cols.shape[0], high.shape[0]
    wide = cols.shape[2]
    near = (side_pieces - 1) * wide
    copies = [pltpu.make_async_copy(factor_part, factor_out, sems.at[0])]
    at = (pl.ds(0, near), pl.ds(0, (count - 1) * wide))
    copies.append(pltpu.make_async_copy(held.at[at], front_out.at[at], sems.at[1]))
    for copy in copies:
        copy.start()

    def update(j, c):
        rows, columns = slice(j * wide, (j + 1) * wide), slice(c * wide, (c + 1) * wide)
        change = contract_rows(high[j], cols[c]) + contract_rows(low[j], cols[c])
        done[rows, columns] = held[rows, columns] - change
        at = (pl.ds(j * wide, wide), pl.ds(c * wide, wide))
        copies.append(pltpu.make_async_copy(done.at[at], front_out.at[at], sems.at[len(copies)]))
        copies[-1].start()

    for j in range(side_pieces - 1):
        update(j, count - 1)
    for c in range(count):
        update(side_pieces - 1, c)
    for copy in copies:
        copy.wait()


def local_kernels(lines, grids, design_panel, design_front, arc_ids, arc_weight, row_counts, panel_inverse, front):
    bf16 = jnp.bfloat16
    slab, whole = panel_inverse.shape
    rows, width = design_panel.shape
    cols = design_front.shape[1]
    tile_rows = front.shape[0]
    side = whole // 2
    share = slab // grids
    wide = tile_rows // 3
    count = cols // wide
    vmem = pl.BlockSpec(memory_space=pltpu.VMEM)
    smem = pl.BlockSpec(memory_space=pltpu.SMEM)
    hbm = pl.BlockSpec(memory_space=pltpu.HBM)
    dma = pltpu.SemaphoreType.DMA
    hops = lines - 1
    arcs = arc_weight.shape[0]

    def stay(value):
        return pltpu.with_memory_space_constraint(value, pltpu.HBM)

    units = grids * count
    slots = units // 2
    f32 = jnp.float32
    outs = pl.pallas_call(
        exchange,
        out_shape=(
            jax.ShapeDtypeStruct((count, whole, wide), bf16),
            jax.ShapeDtypeStruct((3, whole, wide), bf16),
            jax.ShapeDtypeStruct((3, whole, wide), bf16),
            jax.ShapeDtypeStruct(front.shape, f32),
            jax.ShapeDtypeStruct((slab, cols), f32),
        ),
        in_specs=[hbm, hbm, hbm, hbm, smem, hbm, hbm],
        out_specs=(vmem,) * 5,
        scratch_shapes=[
            pltpu.VMEM((count, whole, wide), bf16),
            pltpu.VMEM((3, whole, wide), bf16),
            pltpu.VMEM((2, lines, grids, share, side + 128), bf16),
            pltpu.VMEM((lines, grids, share, side), bf16),
            pltpu.VMEM((rows // arcs, arcs), jnp.int32),
            pltpu.VMEM((1, arcs), f32),
            pltpu.VMEM((slab, whole), f32),
            pltpu.VMEM((grids, rows, width), bf16),
            pltpu.VMEM((rows, cols), bf16),
            pltpu.VMEM((rows, 1), f32),
            pltpu.VMEM((count, grids * width, wide), bf16),
            pltpu.VMEM((count, grids * width, wide), bf16),
            pltpu.VMEM((count, grids * width, wide), bf16),
            pltpu.VMEM((count, grids * width, wide), f32),
            dma((count,)), dma((5,)), dma((4,)), dma((4,)),
            dma((units,)), dma((units,)), dma((units,)), dma((units,)),
            dma((units,)), dma((units,)), dma((units,)), dma((units,)),
            dma((3, slots)), dma((2, slots)), dma((2, slots)),
            dma((3, 2, hops)), dma((3, 2, hops)), dma((3, 4)), dma((3, 4)), dma((3,)), dma((3,)),
        ],
        compiler_params=pltpu.CompilerParams(
            collective_id=0, has_side_effects=True, vmem_limit_bytes=30 * 2**20
        ),
        name="exchange",
    )(stay(design_panel), stay(design_front), stay(arc_ids.reshape((rows // arcs, arcs))),
      stay(arc_weight[None, :]), row_counts, stay(panel_inverse), stay(front))
    return pl.pallas_call(
        finish,
        out_shape=(
            jax.ShapeDtypeStruct((slab, cols), f32),
            jax.ShapeDtypeStruct(front.shape, f32),
        ),
        in_specs=[vmem] * 5,
        out_specs=(hbm, hbm),
        scratch_shapes=[
            pltpu.VMEM(front.shape, f32),
            dma((count + 4,)),
        ],
        compiler_params=pltpu.CompilerParams(vmem_limit_bytes=12 * 2**20),
        name="finish",
    )(*outs)


def solution(mesh):
    placed = (
        P("obs", ("team", "grid")),
        P("obs", "grid"),
        P("obs"),
        P(),
        P("obs"),
        P(("team", "obs"), None),
        P(("team", "obs"), "grid"),
    )
    sizes = mesh.shape
    fits = sizes["team"] == 2 and sizes["obs"] == 4 and sizes["grid"] == 4
    return jax.shard_map(
        functools.partial(local_kernels, sizes["obs"], sizes["grid"]) if fits else local,
        mesh=mesh,
        in_specs=placed,
        out_specs=(P(("team", "obs"), "grid"), P(("team", "obs"), "grid")),
        check_vma=False,
    )
```

```python
import functools

import jax
import jax.numpy as jnp
from jax import lax
from jax.experimental import pallas as pl
from jax.experimental.pallas import tpu as pltpu
from jax.sharding import PartitionSpec as P


def live_weights(arc_ids, arc_weight, row_counts):
    row_total = arc_ids.shape[0]
    arc_total = arc_weight.shape[0]
    hit = arc_ids[:, None] == lax.broadcasted_iota(jnp.int32, (row_total, arc_total), 1)
    looked = jnp.sum(jnp.where(hit, arc_weight[None, :], 0.0), axis=1)
    is_live = lax.broadcasted_iota(jnp.int32, (row_total,), 0) < row_counts[0]
    return looked * is_live.astype(jnp.float32)


def contract_rows(left, right):
    return lax.dot_general(
        left, right, (((0,), (0,)), ((), ())), preferred_element_type=jnp.float32
    )


def local(design_panel, design_front, arc_ids, arc_weight, row_counts, panel_inverse, front):
    high = lax.reduce_precision(panel_inverse, 8, 7)
    split = jnp.concatenate([high, panel_inverse - high], axis=1).astype(jnp.bfloat16)
    inverse_whole = lax.all_gather(split, ("team", "obs"), axis=0, tiled=True)
    weights = live_weights(arc_ids, arc_weight, row_counts)
    scaled_front = (design_front.astype(jnp.float32) * weights[:, None]).astype(jnp.bfloat16)
    panel_piece = lax.all_gather(design_panel, "grid", axis=1, tiled=True)
    partial_value = contract_rows(panel_piece, scaled_front)
    slab_rows = panel_inverse.shape[0]
    place_index = lax.axis_index(("team", "obs"))
    block_part = lax.psum_scatter(partial_value, "obs", scatter_dimension=0, tiled=True)
    block_part = block_part.astype(jnp.bfloat16)
    block_whole = lax.all_gather(block_part, ("team", "obs"), axis=0, tiled=True)
    factor_cols = jnp.dot(
        inverse_whole,
        jnp.concatenate([block_whole, block_whole], axis=0),
        preferred_element_type=jnp.float32,
    )
    factor_part = lax.dynamic_slice_in_dim(factor_cols, place_index * slab_rows, slab_rows, 0)
    factor_cols = factor_cols.astype(jnp.bfloat16)
    tile_rows = front.shape[0]
    tile_ratio = factor_cols.shape[1] // tile_rows
    offset = place_index % tile_ratio * tile_rows
    own_slice = lax.dynamic_slice_in_dim(factor_cols, offset, tile_rows, 1)
    kept = jnp.where(lax.axis_index("grid") == place_index // tile_ratio, own_slice, 0)
    factor_rows = lax.psum(kept.astype(jnp.bfloat16), "grid")
    return (factor_part, front - contract_rows(factor_rows, factor_cols))


MESH = pl.DeviceIdType.MESH


DIRECT = 18
UNITS = (
    (0, 0), (0, 3), (0, 1), (0, 4), (0, 2), (0, 5), (1, 0), (1, 3), (1, 1), (1, 4), (2, 0), (2, 3), (2, 1),
    (2, 4), (3, 0), (3, 3), (3, 1), (3, 4), (1, 2), (2, 2), (3, 2), (1, 5), (2, 5), (3, 5)
)
INNER = (
    (0, 0, 4), (0, 1, 5), (0, 2, 6), (0, 3, 8), (1, 0, 8), (0, 4, 9), (1, 1, 9), (0, 5, 10), (1, 2, 10), (0,
    6, 10), (1, 3, 11), (0, 7, 12), (1, 4, 12), (0, 8, 14), (1, 5, 14), (0, 9, 14), (1, 6, 14), (0, 10, 14),
    (1, 7, 14), (0, 11, 15), (1, 8, 15), (0, 12, 16), (1, 9, 17), (0, 13, 18), (1, 10, 18), (0, 14, 19), (1,
    11, 20), (2, 0, 20), (2, 1, 20), (0, 15, 21), (1, 12, 21), (2, 2, 21), (2, 3, 21), (0, 16, 22), (1, 13,
    22), (2, 4, 22), (2, 5, 22), (0, 17, 23), (1, 14, 23), (2, 6, 24), (0, 18, 24), (2, 7, 24), (1, 15, 24),
    (2, 8, 25), (2, 9, 25), (0, 19, 27), (1, 16, 28), (2, 10, 28), (2, 11, 28), (0, 20, 30), (1, 17, 31), (2,
    12, 31), (2, 13, 31), (0, 21, 32), (1, 18, 34), (2, 14, 35), (2, 15, 35), (0, 22, 36), (1, 19, 37), (2,
    16, 39), (0, 23, 40), (1, 20, 40), (2, 17, 40), (1, 21, 40), (1, 22, 40), (1, 23, 45)
)
OUTER = (
    (1, 0, 12), (1, 1, 14), (1, 2, 14), (1, 3, 14), (1, 4, 14), (1, 5, 17), (1, 6, 19), (1, 7, 21), (2, 0,
    22), (2, 1, 22), (1, 8, 22), (2, 2, 24), (2, 3, 24), (1, 9, 24), (2, 4, 24), (2, 5, 24), (1, 10, 24), (2,
    6, 24), (2, 7, 24), (1, 11, 24), (2, 8, 24), (1, 12, 24), (2, 9, 24), (1, 13, 24), (2, 10, 24), (1, 14,
    24), (2, 11, 24), (1, 15, 24), (2, 12, 26), (1, 16, 29), (2, 13, 30), (1, 17, 32), (2, 14, 34), (1, 18,
    37), (2, 15, 38), (1, 19, 40), (2, 16, 40), (1, 20, 40), (2, 17, 40), (1, 21, 40), (1, 22, 44), (1, 23,
    46)
)


def exchange(
    panel, front_cols, ids_hbm, arc_hbm, counts, inverse_hbm, front,
    cols, high, low, held, factor_part,
    blk, tile, inv_diag, inv_off, ids, arc_weight, inverse_rows,
    panels, scaled, weights, outgoing, from_outer, from_inner, own,
    front_sem, local_sem, panel_send, panel_recv, outer_send, outer_recv, inner_send, inner_recv,
    total_send, total_recv, team_send, team_recv, tile_send, relay_send, tile_recv,
    inv_line_send, inv_line_recv, inv_grid_send, inv_grid_recv, inv_team_send, inv_team_recv,
):
    team, z, grid = lax.axis_index("team"), lax.axis_index("obs"), lax.axis_index("grid")
    rows, width = panel.shape
    lines = inv_diag.shape[1]
    share = inv_diag.shape[3]
    side = inv_off.shape[3]
    x, y = lax.rem(grid, 2), lax.div(grid, 2)
    beside_x = y * 2 + (1 - x)
    beside_y = (1 - y) * 2 + x
    across = (1 - y) * 2 + (1 - x)
    partner = 1 - team
    is_inner = (z == 1) | (z == 2)
    is_outer = jnp.logical_not(is_inner)
    mate = jnp.where(z < 2, 1 - z, 5 - z)
    other = jnp.clip(3 - z, 1, 2)
    half = lax.rem(z, 2)
    root_x = lax.div(z, 2)
    owner = y
    sends_tile = x == root_x
    root_y = team
    at_x = (x != root_x) & (y == root_y)

    barrier = pltpu.get_barrier_semaphore()
    for where in (
        {"grid": beside_x}, {"grid": beside_y}, {"team": partner}, {"obs": mate},
        {"team": partner, "grid": beside_x}, {"team": partner, "grid": beside_y},
        {"grid": across}, {"team": partner, "grid": across},
    ):
        pl.semaphore_signal(barrier, inc=1, device_id=where, device_id_type=MESH)

    @pl.when(is_inner)
    def _():
        pl.semaphore_signal(barrier, inc=1, device_id={"obs": other}, device_id_type=MESH)

    count, side_pieces = blk.shape[0], tile.shape[0]
    wide = blk.shape[2]

    def load_front(c):
        at = (slice(None), pl.ds(c * wide, wide))
        return pltpu.make_async_copy(front_cols.at[at], scaled.at[at], front_sem.at[c])

    load_inverse = pltpu.make_async_copy(inverse_hbm, inverse_rows, local_sem.at[0])
    load_ids = pltpu.make_async_copy(ids_hbm, ids, local_sem.at[1])
    load_arcs = pltpu.make_async_copy(arc_hbm, arc_weight, local_sem.at[2])
    load_panel = pltpu.make_async_copy(panel, panels.at[0], local_sem.at[3])
    load_held = pltpu.make_async_copy(front, held, local_sem.at[4])
    load_inverse.start()
    load_ids.start()
    load_arcs.start()
    load_front(0).start()
    load_panel.start()
    for r, c in UNITS[1:count]:
        load_front(c).start()
    load_held.start()

    step = rows // 8
    load_inverse.wait()
    mine = inverse_rows[pl.ds(pl.multiple_of(grid * share, share), share), :]
    rounded = mine.astype(jnp.bfloat16)
    row_at = lax.broadcasted_iota(jnp.int32, mine.shape, 0) + (team * side + z * width + grid * share)
    on_diagonal = lax.broadcasted_iota(jnp.int32, mine.shape, 1) == row_at
    rest = jnp.sum(jnp.where(on_diagonal, mine - rounded.astype(jnp.float32), 0.0), axis=1, keepdims=True)
    rest = jnp.broadcast_to(rest, (share, inv_diag.shape[4] - side)).astype(jnp.bfloat16)

    @pl.when(team == 0)
    def _():
        inv_diag[0, z, grid, :, :side] = rounded[:, :side]

    @pl.when(team == 1)
    def _():
        inv_diag[1, z, grid, :, :side] = rounded[:, side:]
        inv_off[z, grid] = rounded[:, :side]

    inv_diag[team, z, grid, :, side:] = rest

    pl.semaphore_wait(barrier, jnp.where(is_inner, 9, 8))

    def remote(src, dst, send, recv, where):
        return pltpu.make_async_remote_copy(
            src_ref=src, dst_ref=dst, send_sem=send, recv_sem=recv,
            device_id=where, device_id_type=MESH,
        )

    def await_on(ref, sem):
        pltpu.make_async_copy(ref, ref, sem).wait()

    first = jnp.where(team == 0, beside_x, beside_y)
    second = jnp.where(team == 0, beside_y, beside_x)
    top, bottom = pl.ds(0, rows // 2), pl.ds(rows // 2, rows // 2)
    panel_copies = [
        remote(panel, panels.at[1], panel_send.at[0], panel_recv.at[0], {"grid": first}),
        remote(panel, panels.at[2], panel_send.at[1], panel_recv.at[1], {"grid": second}),
        remote(panels.at[1, top], panels.at[3, top], panel_send.at[2], panel_recv.at[2], {"grid": second}),
        remote(panels.at[2, bottom], panels.at[3, bottom], panel_send.at[3], panel_recv.at[3], {"grid": first}),
    ]
    panel_copies[0].start()

    inv_parts = (
        (0, team == 0, lambda *at: inv_diag.at[(0,) + at]),
        (1, team == 1, lambda *at: inv_diag.at[(1,) + at]),
        (2, team == 1, lambda *at: inv_off.at[at]),
    )

    def inv_line(s, what):
        for k, has, of in inv_parts:
            for d, hop in ((0, 1), (1, -1)):
                held = z - hop * s
                sends = (held >= 0) & (held < lines) & (z + hop >= 0) & (z + hop < lines)
                came = z - hop * (s + 1)
                comes = (came >= 0) & (came < lines)
                if what == "start":
                    @pl.when(has & sends)
                    def _():
                        ref = of(jnp.clip(held, 0, lines - 1), grid)
                        remote(ref, ref, inv_line_send.at[k, d, s], inv_line_recv.at[k, d, s],
                               {"obs": jnp.clip(z + hop, 0, lines - 1)}).start()
                elif what == "wait":
                    @pl.when(has & comes)
                    def _():
                        await_on(of(jnp.clip(came, 0, lines - 1), grid), inv_line_recv.at[k, d, s])
                else:
                    @pl.when(has & sends)
                    def _():
                        await_on(of(jnp.clip(held, 0, lines - 1), grid), inv_line_send.at[k, d, s])

    def inv_grid(stage, what):
        every, first, last = pl.ds(0, lines), pl.ds(0, lines // 2), pl.ds(lines // 2, lines // 2)
        for k, has, of in inv_parts:
            moves = (
                (0, (every, grid), (every, beside_x), {"grid": beside_x}),
                (1, (every, grid), (every, beside_y), {"grid": beside_y}),
            ) if stage == 0 else (
                (2, (first, beside_x), (first, across), {"grid": beside_y}),
                (3, (last, beside_y), (last, across), {"grid": beside_x}),
            )

            @pl.when(has)
            def _():
                for j, sent, came, where in moves:
                    if what == "start":
                        remote(of(*sent), of(*sent), inv_grid_send.at[k, j], inv_grid_recv.at[k, j], where).start()
                    elif what == "wait":
                        await_on(of(*came), inv_grid_recv.at[k, j])
                    else:
                        await_on(of(*sent), inv_grid_send.at[k, j])

    def inv_team(what):
        for k, has, of in inv_parts:
            @pl.when(has)
            def _():
                if what == "start":
                    remote(of(), of(), inv_team_send.at[k], inv_team_recv.at[k], {"team": partner}).start()
                elif what == "drain":
                    await_on(of(), inv_team_send.at[k])

            if what == "wait":
                @pl.when(jnp.logical_not(has))
                def _():
                    await_on(of(), inv_team_recv.at[k])

    inv_line(0, "start")

    arcs = arc_weight.shape[1]
    live = counts[0]
    load_ids.wait()
    load_arcs.wait()
    lane = lax.broadcasted_iota(jnp.int32, (arcs, arcs), 1)
    place_of = lax.broadcasted_iota(jnp.int32, (arcs, arcs), 0)

    def upright(line):
        return jnp.sum(jnp.where(lane == place_of, line, 0), axis=1, keepdims=True)

    arc_column = upright(arc_weight[...])
    for i in range(rows // arcs):
        hit = ids[i:i + 1, :] == place_of
        looked = jnp.sum(jnp.where(hit, arc_column, 0.0), axis=0, keepdims=True)
        slot = lax.broadcasted_iota(jnp.int32, (1, arcs), 1) + i * arcs
        weights[i * arcs:(i + 1) * arcs, :] = jnp.broadcast_to(upright(jnp.where(slot < live, looked, 0.0)), (arcs, arcs))

    def scale(c):
        at_cols = slice(c * wide, (c + 1) * wide)
        load_front(c).wait()

        @pl.loop(0, rows // step)
        def _(i):
            at = pl.ds(pl.multiple_of(i * step, step), step)
            factor = jnp.concatenate([weights[at, :]] * (wide // weights.shape[1]), axis=1)
            part = scaled[at, at_cols].astype(jnp.float32)
            scaled[at, at_cols] = (part * factor).astype(jnp.bfloat16)

    def source(t, r):
        if r == 0:
            return grid
        if r == 3:
            return across
        return jnp.where(t == r - 1, beside_x, beside_y)

    def tile_source(t, r):
        root = root_y * 2 + root_x
        flip_x = root_y * 2 + (1 - root_x)
        flip_y = (1 - root_y) * 2 + root_x
        both = (1 - root_y) * 2 + (1 - root_x)
        return (root, (flip_x, flip_y)[t], (flip_y, flip_x)[t], both)[r]

    def staged(r, c):
        return c, pl.ds(r * width, width)

    def block_rows(t, g):
        return pl.ds(pl.multiple_of((t * 4 + g) * width, width), width)

    def place(t, r, c):
        return c, block_rows(t, source(t, r))

    def tile_place(t, r, c):
        return c % side_pieces, block_rows(t, tile_source(t, r))

    def slot_of(r, c):
        return r * side_pieces + c % side_pieces

    def in_half(c):
        return half == c // side_pieces

    def compute(u):
        r, c = UNITS[u]
        if r == 0:
            scale(c)
        total = contract_rows(panels[r], scaled[:, c * wide:(c + 1) * wide])
        at = staged(r, c)

        @pl.when(is_inner)
        def _():
            own[at] = total

        @pl.when(is_outer)
        def _():
            outgoing[at] = total.astype(jnp.bfloat16)
            remote(outgoing.at[at], from_outer.at[at], outer_send.at[u], outer_recv.at[u], {"obs": mate}).start()

    def middle(u):
        at = staged(*UNITS[u])
        await_on(from_outer.at[at], outer_recv.at[u])
        total = own[at] + from_outer[at].astype(jnp.float32)
        own[at] = total
        outgoing[at] = total.astype(jnp.bfloat16)
        remote(outgoing.at[at], from_inner.at[at], inner_send.at[u], inner_recv.at[u], {"obs": other}).start()

    def spread_tile(u):
        r, c = UNITS[u]
        ref = blk.at[place(team, r, c)]

        @pl.when(sends_tile & in_half(c))
        def _():
            k = slot_of(r, c)
            to = tile.at[c % side_pieces, block_rows(team, source(team, r))]
            remote(ref, to, tile_send.at[0, k], tile_recv.at[team, k], {"team": owner, "grid": beside_x}).start()
            remote(ref, to, tile_send.at[1, k], tile_recv.at[team, k], {"team": owner, "grid": beside_y}).start()
            if u >= DIRECT:
                remote(ref, to, tile_send.at[3, k], tile_recv.at[team, k], {"team": owner, "grid": across}).start()

            @pl.when(team == owner)
            def _():
                pltpu.make_async_copy(ref, to, tile_recv.at[team, k]).start()

            @pl.when(team != owner)
            def _():
                remote(ref, to, tile_send.at[2, k], tile_recv.at[team, k], {"team": partner}).start()

    def spread(u):
        ref = blk.at[place(team, *UNITS[u])]
        if u >= count:
            spread_tile(u)
        remote(ref, ref, team_send.at[u], team_recv.at[u], {"team": partner}).start()

    def finished_inner(u):
        r, c = UNITS[u]
        at = staged(r, c)
        await_on(from_inner.at[at], inner_recv.at[u])
        total = own[at] + from_inner[at].astype(jnp.float32)
        spot = place(team, r, c)
        blk[spot] = total.astype(jnp.bfloat16)
        ref = blk.at[spot]
        remote(ref, ref, total_send.at[u], total_recv.at[u], {"obs": mate}).start()
        spread(u)

    def finished_outer(u):
        await_on(blk.at[place(team, *UNITS[u])], total_recv.at[u])
        spread(u)

    def relay(u):
        r, c = UNITS[u]
        k = slot_of(r, c)

        @pl.when(at_x & in_half(c))
        def _():
            for t in (0, 1):
                ref = tile.at[tile_place(t, r, c)]
                await_on(ref, tile_recv.at[t, k])
                remote(ref, ref, relay_send.at[t, k], tile_recv.at[t, k], {"grid": beside_y}).start()

    slab = inverse_rows.shape[0]
    size = 2 * slab
    blocks = blk.shape[1] // size
    pair = team * lines + z

    def factor_of(ref, c, r):
        t, inner = r * size // side, r * size % side
        begin, near = inner // slab, slice(r * size, (r + 1) * size)
        ahead = inv_diag[t, begin:begin + 2].reshape((size, inv_diag.shape[4]))
        total = ahead[:, side:side + 1].astype(jnp.float32) * ref[c, near].astype(jnp.float32)
        total += jnp.dot(
            ahead[:, :inner + size], ref[c, t * side:t * side + inner + size],
            preferred_element_type=jnp.float32,
        )
        if t:
            behind = inv_off[begin:begin + 2].reshape((size, side))
            total += jnp.dot(behind, ref[c, :side], preferred_element_type=jnp.float32)
        return total

    def factor_columns(c, r):
        if r == 0:
            for u in range(len(UNITS)):
                if UNITS[u][1] == c:
                    await_on(blk.at[place(partner, *UNITS[u])], team_recv.at[u])
        value = factor_of(blk, c, r)
        cols[c, r * size:(r + 1) * size] = value.astype(jnp.bfloat16)
        for part in range(size // slab):
            @pl.when(pair == r * (size // slab) + part)
            def _():
                factor_part[:, c * wide:(c + 1) * wide] = value[part * slab:(part + 1) * slab]

    def factor_tile(j, r):
        if r == 0:
            for u, (d, c) in enumerate(UNITS):
                if c % side_pieces == j:
                    @pl.when(in_half(c) & (jnp.logical_not(at_x) | (u >= DIRECT)))
                    def _():
                        for t in (0, 1):
                            await_on(tile.at[tile_place(t, d, c)], tile_recv.at[t, slot_of(d, c)])
        value = factor_of(tile, j, r)
        upper = value.astype(jnp.bfloat16)
        high[j, r * size:(r + 1) * size] = upper
        low[j, r * size:(r + 1) * size] = (value - upper.astype(jnp.float32)).astype(jnp.bfloat16)

    def update(c, j):
        near, at = slice(j * wide, (j + 1) * wide), slice(c * wide, (c + 1) * wide)
        change = contract_rows(high[j], cols[c]) + contract_rows(low[j], cols[c])
        held[near, at] = held[near, at] - change

    last = len(UNITS)
    work = [(compute, (u,)) for u in range(last)]

    def columns_work(c):
        return [(factor_columns, (c, r)) for r in range(blocks)]

    def tile_work(j):
        return [(factor_tile, (j, r)) for r in range(blocks)]

    def update_work(cs, js):
        return [(update, (c, j)) for j in js for c in cs]

    work += columns_work(0) + columns_work(3) + columns_work(1) + columns_work(4)
    work += tile_work(0) + update_work((0, 3, 1, 4), (0,))
    work += tile_work(1) + update_work((0, 3), (1,)) + columns_work(2) + update_work((1, 4), (1,))
    work += update_work((2,), (0, 1)) + columns_work(5) + tile_work(2)
    early = max(at for kind, u, at in INNER + OUTER if kind == 1 and u < count)
    starts = [min(u for u in range(last) if UNITS[u][0] == r) for r in range(4)]

    def hooks(i):
        if i == 0:
            load_panel.wait()
        if i == 2:
            inv_line(0, "wait")
            inv_line(1, "start")
        if i == 4:
            inv_line(1, "wait")
            inv_line(2, "start")
        if i == 3:
            panel_copies[1].start()
        if i == starts[1]:
            inv_line(2, "wait")
            panel_copies[0].wait_recv()
            panel_copies[2].start()
        if i == starts[2]:
            panel_copies[1].wait_recv()
            panel_copies[3].start()
            inv_grid(0, "start")
        if i == starts[3]:
            panel_copies[2].wait_recv()
            panel_copies[3].wait_recv()
        if i == early:
            for u in range(count):
                spread_tile(u)
        if i == starts[3] + 5:
            inv_grid(0, "wait")
            inv_grid(1, "start")
        if i == starts[3] + 8:
            inv_grid(1, "wait")
            inv_team("start")
        if i == last:
            inv_team("wait")
        if i == last + 5 * blocks:
            load_held.wait()

    def role_work(steps, functions, i):
        for kind, u, at in steps:
            if at == i:
                functions[kind](u)

    for i in range(len(work) + 1):
        if any(at == i for _, _, at in INNER):
            @pl.when(is_inner)
            def _():
                role_work(INNER, (middle, finished_inner, relay), i)

        if any(at == i for _, _, at in OUTER):
            @pl.when(is_outer)
            def _():
                role_work(OUTER, (None, finished_outer, relay), i)

        hooks(i)
        if i < len(work):
            function, at = work[i]
            function(*at)

    for copy in panel_copies:
        copy.wait_send()
    for s in range(lines - 1):
        inv_line(s, "drain")
    inv_grid(0, "drain")
    inv_grid(1, "drain")
    inv_team("drain")
    for u in range(last):
        r, c = UNITS[u]
        k = slot_of(r, c)
        at = staged(r, c)
        ref = blk.at[place(team, r, c)]
        await_on(ref, team_send.at[u])

        @pl.when(is_outer)
        def _():
            await_on(outgoing.at[at], outer_send.at[u])

        @pl.when(is_inner)
        def _():
            await_on(outgoing.at[at], inner_send.at[u])
            await_on(ref, total_send.at[u])

        @pl.when(in_half(c) & sends_tile)
        def _():
            await_on(ref, tile_send.at[0, k])
            await_on(ref, tile_send.at[1, k])
            if u >= DIRECT:
                await_on(ref, tile_send.at[3, k])

            @pl.when(team != owner)
            def _():
                await_on(ref, tile_send.at[2, k])

        if u < DIRECT:
            @pl.when(in_half(c) & at_x)
            def _():
                for t in (0, 1):
                    await_on(tile.at[tile_place(t, r, c)], relay_send.at[t, k])


def finish(cols, high, low, held, factor_part, factor_out, front_out, done, sems):
    count, side_pieces = cols.shape[0], high.shape[0]
    wide = cols.shape[2]
    near = (side_pieces - 1) * wide
    copies = [pltpu.make_async_copy(factor_part, factor_out, sems.at[0])]
    at = (pl.ds(0, near), pl.ds(0, (count - 1) * wide))
    copies.append(pltpu.make_async_copy(held.at[at], front_out.at[at], sems.at[1]))
    for copy in copies:
        copy.start()

    def update(j, c):
        rows, columns = slice(j * wide, (j + 1) * wide), slice(c * wide, (c + 1) * wide)
        change = contract_rows(high[j], cols[c]) + contract_rows(low[j], cols[c])
        done[rows, columns] = held[rows, columns] - change
        at = (pl.ds(j * wide, wide), pl.ds(c * wide, wide))
        copies.append(pltpu.make_async_copy(done.at[at], front_out.at[at], sems.at[len(copies)]))
        copies[-1].start()

    for j in range(side_pieces - 1):
        update(j, count - 1)
    for c in range(count):
        update(side_pieces - 1, c)
    for copy in copies:
        copy.wait()


def local_kernels(lines, grids, design_panel, design_front, arc_ids, arc_weight, row_counts, panel_inverse, front):
    bf16 = jnp.bfloat16
    slab, whole = panel_inverse.shape
    rows, width = design_panel.shape
    cols = design_front.shape[1]
    tile_rows = front.shape[0]
    side = whole // 2
    share = slab // grids
    wide = tile_rows // 3
    count = cols // wide
    vmem = pl.BlockSpec(memory_space=pltpu.VMEM)
    smem = pl.BlockSpec(memory_space=pltpu.SMEM)
    hbm = pl.BlockSpec(memory_space=pltpu.HBM)
    dma = pltpu.SemaphoreType.DMA
    hops = lines - 1
    arcs = arc_weight.shape[0]

    def stay(value):
        return pltpu.with_memory_space_constraint(value, pltpu.HBM)

    units = grids * count
    slots = units // 2
    f32 = jnp.float32
    outs = pl.pallas_call(
        exchange,
        out_shape=(
            jax.ShapeDtypeStruct((count, whole, wide), bf16),
            jax.ShapeDtypeStruct((3, whole, wide), bf16),
            jax.ShapeDtypeStruct((3, whole, wide), bf16),
            jax.ShapeDtypeStruct(front.shape, f32),
            jax.ShapeDtypeStruct((slab, cols), f32),
        ),
        in_specs=[hbm, hbm, hbm, hbm, smem, hbm, hbm],
        out_specs=(vmem,) * 5,
        scratch_shapes=[
            pltpu.VMEM((count, whole, wide), bf16),
            pltpu.VMEM((3, whole, wide), bf16),
            pltpu.VMEM((2, lines, grids, share, side + 128), bf16),
            pltpu.VMEM((lines, grids, share, side), bf16),
            pltpu.VMEM((rows // arcs, arcs), jnp.int32),
            pltpu.VMEM((1, arcs), f32),
            pltpu.VMEM((slab, whole), f32),
            pltpu.VMEM((grids, rows, width), bf16),
            pltpu.VMEM((rows, cols), bf16),
            pltpu.VMEM((rows, arcs), f32),
            pltpu.VMEM((count, grids * width, wide), bf16),
            pltpu.VMEM((count, grids * width, wide), bf16),
            pltpu.VMEM((count, grids * width, wide), bf16),
            pltpu.VMEM((count, grids * width, wide), f32),
            dma((count,)), dma((5,)), dma((4,)), dma((4,)),
            dma((units,)), dma((units,)), dma((units,)), dma((units,)),
            dma((units,)), dma((units,)), dma((units,)), dma((units,)),
            dma((4, slots)), dma((2, slots)), dma((2, slots)),
            dma((3, 2, hops)), dma((3, 2, hops)), dma((3, 4)), dma((3, 4)), dma((3,)), dma((3,)),
        ],
        compiler_params=pltpu.CompilerParams(
            collective_id=0, has_side_effects=True, vmem_limit_bytes=30 * 2**20
        ),
        name="exchange",
    )(stay(design_panel), stay(design_front), stay(arc_ids.reshape((rows // arcs, arcs))),
      stay(arc_weight[None, :]), row_counts, stay(panel_inverse), stay(front))
    return pl.pallas_call(
        finish,
        out_shape=(
            jax.ShapeDtypeStruct((slab, cols), f32),
            jax.ShapeDtypeStruct(front.shape, f32),
        ),
        in_specs=[vmem] * 5,
        out_specs=(hbm, hbm),
        scratch_shapes=[
            pltpu.VMEM(front.shape, f32),
            dma((count + 4,)),
        ],
        compiler_params=pltpu.CompilerParams(vmem_limit_bytes=12 * 2**20),
        name="finish",
    )(*outs)


def solution(mesh):
    placed = (
        P("obs", ("team", "grid")),
        P("obs", "grid"),
        P("obs"),
        P(),
        P("obs"),
        P(("team", "obs"), None),
        P(("team", "obs"), "grid"),
    )
    sizes = mesh.shape
    fits = sizes["team"] == 2 and sizes["obs"] == 4 and sizes["grid"] == 4
    return jax.shard_map(
        functools.partial(local_kernels, sizes["obs"], sizes["grid"]) if fits else local,
        mesh=mesh,
        in_specs=placed,
        out_specs=(P(("team", "obs"), "grid"), P(("team", "obs"), "grid")),
        check_vma=False,
    )
```

```python
import functools

import jax
import jax.numpy as jnp
from jax import lax
from jax.experimental import pallas as pl
from jax.experimental.pallas import tpu as pltpu
from jax.sharding import PartitionSpec as P


def live_weights(arc_ids, arc_weight, row_counts):
    row_total = arc_ids.shape[0]
    arc_total = arc_weight.shape[0]
    hit = arc_ids[:, None] == lax.broadcasted_iota(jnp.int32, (row_total, arc_total), 1)
    looked = jnp.sum(jnp.where(hit, arc_weight[None, :], 0.0), axis=1)
    is_live = lax.broadcasted_iota(jnp.int32, (row_total,), 0) < row_counts[0]
    return looked * is_live.astype(jnp.float32)


def contract_rows(left, right):
    return lax.dot_general(
        left, right, (((0,), (0,)), ((), ())), preferred_element_type=jnp.float32
    )


def local(design_panel, design_front, arc_ids, arc_weight, row_counts, panel_inverse, front):
    high = lax.reduce_precision(panel_inverse, 8, 7)
    split = jnp.concatenate([high, panel_inverse - high], axis=1).astype(jnp.bfloat16)
    inverse_whole = lax.all_gather(split, ("team", "obs"), axis=0, tiled=True)
    weights = live_weights(arc_ids, arc_weight, row_counts)
    scaled_front = (design_front.astype(jnp.float32) * weights[:, None]).astype(jnp.bfloat16)
    panel_piece = lax.all_gather(design_panel, "grid", axis=1, tiled=True)
    partial_value = contract_rows(panel_piece, scaled_front)
    slab_rows = panel_inverse.shape[0]
    place_index = lax.axis_index(("team", "obs"))
    block_part = lax.psum_scatter(partial_value, "obs", scatter_dimension=0, tiled=True)
    block_part = block_part.astype(jnp.bfloat16)
    block_whole = lax.all_gather(block_part, ("team", "obs"), axis=0, tiled=True)
    factor_cols = jnp.dot(
        inverse_whole,
        jnp.concatenate([block_whole, block_whole], axis=0),
        preferred_element_type=jnp.float32,
    )
    factor_part = lax.dynamic_slice_in_dim(factor_cols, place_index * slab_rows, slab_rows, 0)
    factor_cols = factor_cols.astype(jnp.bfloat16)
    tile_rows = front.shape[0]
    tile_ratio = factor_cols.shape[1] // tile_rows
    offset = place_index % tile_ratio * tile_rows
    own_slice = lax.dynamic_slice_in_dim(factor_cols, offset, tile_rows, 1)
    kept = jnp.where(lax.axis_index("grid") == place_index // tile_ratio, own_slice, 0)
    factor_rows = lax.psum(kept.astype(jnp.bfloat16), "grid")
    return (factor_part, front - contract_rows(factor_rows, factor_cols))


MESH = pl.DeviceIdType.MESH


DIRECT = 18
UNITS = (
    (0, 0), (0, 3), (0, 1), (0, 4), (0, 2), (0, 5), (1, 0), (1, 3), (1, 1), (1, 4), (2, 0), (2, 3), (2, 1),
    (2, 4), (3, 0), (3, 3), (3, 1), (3, 4), (1, 2), (2, 2), (3, 2), (1, 5), (2, 5), (3, 5)
)
INNER = (
    (0, 0, 4), (0, 1, 5), (0, 2, 6), (0, 3, 8), (1, 0, 8), (0, 4, 9), (1, 1, 9), (0, 5, 10), (1, 2, 10), (0,
    6, 10), (1, 3, 11), (0, 7, 12), (1, 4, 12), (0, 8, 14), (1, 5, 14), (0, 9, 14), (1, 6, 14), (0, 10, 14),
    (1, 7, 14), (0, 11, 15), (1, 8, 15), (0, 12, 16), (1, 9, 17), (0, 13, 18), (1, 10, 18), (0, 14, 19), (1,
    11, 20), (2, 0, 20), (2, 1, 20), (0, 15, 21), (1, 12, 21), (2, 2, 21), (2, 3, 21), (0, 16, 22), (1, 13,
    22), (2, 4, 22), (2, 5, 22), (0, 17, 23), (1, 14, 23), (2, 6, 24), (0, 18, 24), (2, 7, 24), (1, 15, 24),
    (2, 8, 25), (2, 9, 25), (0, 19, 27), (1, 16, 28), (2, 10, 28), (2, 11, 28), (0, 20, 30), (1, 17, 31), (2,
    12, 31), (2, 13, 31), (0, 21, 32), (1, 18, 34), (2, 14, 35), (2, 15, 35), (0, 22, 36), (1, 19, 37), (2,
    16, 39), (2, 18, 39), (0, 23, 40), (1, 20, 40), (2, 17, 40), (1, 21, 40), (1, 22, 40), (2, 19, 42), (1,
    23, 45), (2, 20, 45), (2, 21, 45), (2, 22, 45), (2, 23, 50)
)
OUTER = (
    (1, 0, 12), (1, 1, 14), (1, 2, 14), (1, 3, 14), (1, 4, 14), (1, 5, 17), (1, 6, 19), (1, 7, 21), (2, 0,
    22), (2, 1, 22), (1, 8, 22), (2, 2, 24), (2, 3, 24), (1, 9, 24), (2, 4, 24), (2, 5, 24), (1, 10, 24), (2,
    6, 24), (2, 7, 24), (1, 11, 24), (2, 8, 24), (1, 12, 24), (2, 9, 24), (1, 13, 24), (2, 10, 24), (1, 14,
    24), (2, 11, 24), (1, 15, 24), (2, 12, 26), (1, 16, 29), (2, 13, 30), (1, 17, 32), (2, 14, 34), (1, 18,
    37), (2, 15, 38), (1, 19, 40), (2, 16, 40), (1, 20, 40), (2, 17, 40), (1, 21, 40), (2, 18, 42), (1, 22,
    44), (2, 19, 45), (2, 20, 45), (2, 21, 45), (1, 23, 46), (2, 22, 49), (2, 23, 51)
)


def exchange(
    panel, front_cols, ids_hbm, arc_hbm, counts, inverse_hbm, front,
    cols, both, held, factor_part,
    blk, tile, inv_diag, inv_off, ids, arc_weight, inverse_rows,
    panels, scaled, weights, outgoing, from_outer, from_inner, own,
    front_sem, local_sem, panel_send, panel_recv, outer_send, outer_recv, inner_send, inner_recv,
    total_send, total_recv, team_send, team_recv, tile_send, relay_send, tile_recv,
    inv_line_send, inv_line_recv, inv_grid_send, inv_grid_recv, inv_team_send, inv_team_recv,
):
    team, z, grid = lax.axis_index("team"), lax.axis_index("obs"), lax.axis_index("grid")
    rows, width = panel.shape
    lines = inv_diag.shape[1]
    share = inv_diag.shape[3]
    side = inv_off.shape[3]
    x, y = lax.rem(grid, 2), lax.div(grid, 2)
    beside_x = y * 2 + (1 - x)
    beside_y = (1 - y) * 2 + x
    across = (1 - y) * 2 + (1 - x)
    partner = 1 - team
    is_inner = (z == 1) | (z == 2)
    is_outer = jnp.logical_not(is_inner)
    mate = jnp.where(z < 2, 1 - z, 5 - z)
    other = jnp.clip(3 - z, 1, 2)
    half = lax.rem(z, 2)
    root_x = lax.div(z, 2)
    owner = y
    sends_tile = x == root_x
    root_y = team
    at_x = (x != root_x) & (y == root_y)
    straight = root_x == 0

    barrier = pltpu.get_barrier_semaphore()
    for where in (
        {"grid": beside_x}, {"grid": beside_y}, {"team": partner}, {"obs": mate},
        {"team": partner, "grid": beside_x}, {"team": partner, "grid": beside_y},
        {"grid": across}, {"team": partner, "grid": across},
    ):
        pl.semaphore_signal(barrier, inc=1, device_id=where, device_id_type=MESH)

    @pl.when(is_inner)
    def _():
        pl.semaphore_signal(barrier, inc=1, device_id={"obs": other}, device_id_type=MESH)

    count, side_pieces = blk.shape[0], tile.shape[0]
    wide = blk.shape[2]

    def load_front(c):
        at = (slice(None), pl.ds(c * wide, wide))
        return pltpu.make_async_copy(front_cols.at[at], scaled.at[at], front_sem.at[c])

    load_inverse = pltpu.make_async_copy(inverse_hbm, inverse_rows, local_sem.at[0])
    load_ids = pltpu.make_async_copy(ids_hbm, ids, local_sem.at[1])
    load_arcs = pltpu.make_async_copy(arc_hbm, arc_weight, local_sem.at[2])
    load_panel = pltpu.make_async_copy(panel, panels.at[0], local_sem.at[3])
    load_held = pltpu.make_async_copy(front, held, local_sem.at[4])
    load_inverse.start()
    load_ids.start()
    load_arcs.start()
    load_front(0).start()
    load_panel.start()
    for r, c in UNITS[1:count]:
        load_front(c).start()
    load_held.start()

    step = rows // 8
    load_inverse.wait()
    pair_at = jnp.where(team == 0, x, y)
    mine = inverse_rows[pl.ds(pl.multiple_of(pair_at * share, share), share), :]
    rounded = mine.astype(jnp.bfloat16)
    row_at = lax.broadcasted_iota(jnp.int32, mine.shape, 0) + (team * side + z * width + pair_at * share)
    on_diagonal = lax.broadcasted_iota(jnp.int32, mine.shape, 1) == row_at
    rest = jnp.sum(jnp.where(on_diagonal, mine - rounded.astype(jnp.float32), 0.0), axis=1, keepdims=True)
    rest = jnp.broadcast_to(rest, (share, inv_diag.shape[4] - side)).astype(jnp.bfloat16)

    @pl.when(team == 0)
    def _():
        inv_diag[0, z, pair_at, :, :side] = rounded[:, :side]

    @pl.when(team == 1)
    def _():
        inv_diag[1, z, pair_at, :, :side] = rounded[:, side:]
        inv_off[z, pair_at] = rounded[:, :side]

    inv_diag[team, z, pair_at, :, side:] = rest

    pl.semaphore_wait(barrier, jnp.where(is_inner, 9, 8))

    def remote(src, dst, send, recv, where):
        return pltpu.make_async_remote_copy(
            src_ref=src, dst_ref=dst, send_sem=send, recv_sem=recv,
            device_id=where, device_id_type=MESH,
        )

    def await_on(ref, sem):
        pltpu.make_async_copy(ref, ref, sem).wait()

    first = jnp.where(team == 0, beside_x, beside_y)
    second = jnp.where(team == 0, beside_y, beside_x)
    top, bottom = pl.ds(0, rows // 2), pl.ds(rows // 2, rows // 2)
    panel_copies = [
        remote(panel, panels.at[1], panel_send.at[0], panel_recv.at[0], {"grid": first}),
        remote(panel, panels.at[2], panel_send.at[1], panel_recv.at[1], {"grid": second}),
        remote(panels.at[1, top], panels.at[3, top], panel_send.at[2], panel_recv.at[2], {"grid": second}),
        remote(panels.at[2, bottom], panels.at[3, bottom], panel_send.at[3], panel_recv.at[3], {"grid": first}),
    ]
    panel_copies[0].start()

    inv_parts = (
        (0, team == 0, lambda *at: inv_diag.at[(0,) + at]),
        (1, team == 1, lambda *at: inv_diag.at[(1,) + at]),
        (2, team == 1, lambda *at: inv_off.at[at]),
    )

    def inv_line(s, what):
        for k, has, of in inv_parts:
            for d, hop in ((0, 1), (1, -1)):
                held = z - hop * s
                sends = (held >= 0) & (held < lines) & (z + hop >= 0) & (z + hop < lines)
                came = z - hop * (s + 1)
                comes = (came >= 0) & (came < lines)
                if what == "start":
                    @pl.when(has & sends)
                    def _():
                        ref = of(jnp.clip(held, 0, lines - 1), pair_at)
                        remote(ref, ref, inv_line_send.at[k, d, s], inv_line_recv.at[k, d, s],
                               {"obs": jnp.clip(z + hop, 0, lines - 1)}).start()
                elif what == "wait":
                    @pl.when(has & comes)
                    def _():
                        await_on(of(jnp.clip(came, 0, lines - 1), pair_at), inv_line_recv.at[k, d, s])
                else:
                    @pl.when(has & sends)
                    def _():
                        await_on(of(jnp.clip(held, 0, lines - 1), pair_at), inv_line_send.at[k, d, s])

    def inv_grid(what):
        every = pl.ds(0, lines)
        for k, has, of in inv_parts:
            @pl.when(has)
            def _():
                sent, came = of(every, pair_at), of(every, 1 - pair_at)
                if what == "start":
                    remote(sent, sent, inv_grid_send.at[k], inv_grid_recv.at[k], {"grid": first}).start()
                elif what == "wait":
                    await_on(came, inv_grid_recv.at[k])
                else:
                    await_on(sent, inv_grid_send.at[k])

    def inv_team(what):
        for k, has, of in inv_parts:
            @pl.when(has)
            def _():
                if what == "start":
                    remote(of(), of(), inv_team_send.at[k], inv_team_recv.at[k], {"team": partner}).start()
                elif what == "drain":
                    await_on(of(), inv_team_send.at[k])

            if what == "wait":
                @pl.when(jnp.logical_not(has))
                def _():
                    await_on(of(), inv_team_recv.at[k])

    inv_line(0, "start")

    arcs = arc_weight.shape[1]
    live = counts[0]
    load_ids.wait()
    load_arcs.wait()
    lane = lax.broadcasted_iota(jnp.int32, (arcs, arcs), 1)
    place_of = lax.broadcasted_iota(jnp.int32, (arcs, arcs), 0)

    def upright(line):
        return jnp.sum(jnp.where(lane == place_of, line, 0), axis=1, keepdims=True)

    arc_column = upright(arc_weight[...])
    for i in range(rows // arcs):
        hit = ids[i:i + 1, :] == place_of
        looked = jnp.sum(jnp.where(hit, arc_column, 0.0), axis=0, keepdims=True)
        slot = lax.broadcasted_iota(jnp.int32, (1, arcs), 1) + i * arcs
        weights[i * arcs:(i + 1) * arcs, :] = jnp.broadcast_to(upright(jnp.where(slot < live, looked, 0.0)), (arcs, arcs))

    def scale(c):
        at_cols = slice(c * wide, (c + 1) * wide)
        load_front(c).wait()

        @pl.loop(0, rows // step)
        def _(i):
            at = pl.ds(pl.multiple_of(i * step, step), step)
            factor = jnp.concatenate([weights[at, :]] * (wide // weights.shape[1]), axis=1)
            part = scaled[at, at_cols].astype(jnp.float32)
            scaled[at, at_cols] = (part * factor).astype(jnp.bfloat16)

    def source(t, r):
        if r == 0:
            return grid
        if r == 3:
            return across
        return jnp.where(t == r - 1, beside_x, beside_y)

    def tile_source(t, r):
        root = root_y * 2 + root_x
        flip_x = root_y * 2 + (1 - root_x)
        flip_y = (1 - root_y) * 2 + root_x
        both = (1 - root_y) * 2 + (1 - root_x)
        return (root, (flip_x, flip_y)[t], (flip_y, flip_x)[t], both)[r]

    def staged(r, c):
        return c, pl.ds(r * width, width)

    def block_rows(t, g):
        return pl.ds(pl.multiple_of((t * 4 + g) * width, width), width)

    def place(t, r, c):
        return c, block_rows(t, source(t, r))

    def tile_place(t, r, c):
        return c % side_pieces, block_rows(t, tile_source(t, r))

    def slot_of(r, c):
        return r * side_pieces + c % side_pieces

    def in_half(c):
        return half == c // side_pieces

    def relays(u):
        stored = at_x & in_half(UNITS[u][1])
        return stored & jnp.logical_not(straight) if u >= DIRECT else stored

    def compute(u):
        r, c = UNITS[u]
        if r == 0:
            scale(c)
        total = contract_rows(panels[r], scaled[:, c * wide:(c + 1) * wide])
        at = staged(r, c)

        @pl.when(is_inner)
        def _():
            own[at] = total

        @pl.when(is_outer)
        def _():
            outgoing[at] = total.astype(jnp.bfloat16)
            remote(outgoing.at[at], from_outer.at[at], outer_send.at[u], outer_recv.at[u], {"obs": mate}).start()

    def middle(u):
        at = staged(*UNITS[u])
        await_on(from_outer.at[at], outer_recv.at[u])
        total = own[at] + from_outer[at].astype(jnp.float32)
        own[at] = total
        outgoing[at] = total.astype(jnp.bfloat16)
        remote(outgoing.at[at], from_inner.at[at], inner_send.at[u], inner_recv.at[u], {"obs": other}).start()

    def spread_tile(u):
        r, c = UNITS[u]
        ref = blk.at[place(team, r, c)]

        @pl.when(sends_tile & in_half(c))
        def _():
            k = slot_of(r, c)
            to = tile.at[c % side_pieces, block_rows(team, source(team, r))]
            remote(ref, to, tile_send.at[0, k], tile_recv.at[team, k], {"team": owner, "grid": beside_x}).start()
            remote(ref, to, tile_send.at[1, k], tile_recv.at[team, k], {"team": owner, "grid": beside_y}).start()
            if u >= DIRECT:
                @pl.when(straight)
                def _():
                    remote(ref, to, tile_send.at[3, k], tile_recv.at[team, k], {"team": owner, "grid": across}).start()

            @pl.when(team == owner)
            def _():
                pltpu.make_async_copy(ref, to, tile_recv.at[team, k]).start()

            @pl.when(team != owner)
            def _():
                remote(ref, to, tile_send.at[2, k], tile_recv.at[team, k], {"team": partner}).start()

    def spread(u):
        ref = blk.at[place(team, *UNITS[u])]
        if u >= count:
            spread_tile(u)
        remote(ref, ref, team_send.at[u], team_recv.at[u], {"team": partner}).start()

    def finished_inner(u):
        r, c = UNITS[u]
        at = staged(r, c)
        await_on(from_inner.at[at], inner_recv.at[u])
        total = own[at] + from_inner[at].astype(jnp.float32)
        spot = place(team, r, c)
        blk[spot] = total.astype(jnp.bfloat16)
        ref = blk.at[spot]
        remote(ref, ref, total_send.at[u], total_recv.at[u], {"obs": mate}).start()
        spread(u)

    def finished_outer(u):
        await_on(blk.at[place(team, *UNITS[u])], total_recv.at[u])
        spread(u)

    def relay(u):
        r, c = UNITS[u]
        k = slot_of(r, c)

        @pl.when(relays(u))
        def _():
            for t in (0, 1):
                ref = tile.at[tile_place(t, r, c)]
                await_on(ref, tile_recv.at[t, k])
                remote(ref, ref, relay_send.at[t, k], tile_recv.at[t, k], {"grid": beside_y}).start()

    slab = inverse_rows.shape[0]
    size = 2 * slab
    blocks = blk.shape[1] // size
    pair = team * lines + z

    def factor_of(ref, c, t):
        middle_row, begin = side // 2, t * side
        near = inv_diag[t].reshape((side, inv_diag.shape[4]))
        total = near[:, side:side + 1].astype(jnp.float32) * ref[c, begin:begin + side].astype(jnp.float32)
        total += jnp.dot(
            near[:, :middle_row], ref[c, begin:begin + middle_row], preferred_element_type=jnp.float32
        )
        if t:
            total += jnp.dot(
                inv_off[...].reshape((side, side)), ref[c, :side], preferred_element_type=jnp.float32
            )
        lower = total[middle_row:] + jnp.dot(
            near[middle_row:, middle_row:side], ref[c, begin + middle_row:begin + side],
            preferred_element_type=jnp.float32,
        )
        return total[:middle_row], lower

    def factor_columns(c, r):
        if r == 0:
            for u in range(len(UNITS)):
                if UNITS[u][1] == c:
                    await_on(blk.at[place(partner, *UNITS[u])], team_recv.at[u])
        if r % 2 == 0:
            return
        for k, value in enumerate(factor_of(blk, c, r // 2), r - 1):
            cols[c, k * size:(k + 1) * size] = value.astype(jnp.bfloat16)
            for part in range(size // slab):
                @pl.when(pair == k * (size // slab) + part)
                def _():
                    factor_part[:, c * wide:(c + 1) * wide] = value[part * slab:(part + 1) * slab]

    def factor_tile(j, r):
        if r == 0:
            for u, (d, c) in enumerate(UNITS):
                if c % side_pieces == j:
                    @pl.when(in_half(c) & jnp.logical_not(relays(u)))
                    def _():
                        for t in (0, 1):
                            await_on(tile.at[tile_place(t, d, c)], tile_recv.at[t, slot_of(d, c)])
        if r % 2 == 0:
            return
        for k, value in enumerate(factor_of(tile, j, r // 2), r - 1):
            upper = value.astype(jnp.bfloat16)
            both[j, k * size:(k + 1) * size, :wide] = upper
            both[j, k * size:(k + 1) * size, wide:] = (value - upper.astype(jnp.float32)).astype(jnp.bfloat16)

    def update(c, j):
        near, at = slice(j * wide, (j + 1) * wide), slice(c * wide, (c + 1) * wide)
        change = contract_rows(both[j], cols[c])
        held[near, at] = held[near, at] - (change[:wide] + change[wide:])

    last = len(UNITS)
    work = [(compute, (u,)) for u in range(last)]

    def columns_work(c):
        return [(factor_columns, (c, r)) for r in range(blocks)]

    def tile_work(j):
        return [(factor_tile, (j, r)) for r in range(blocks)]

    def update_work(cs, js):
        return [(update, (c, j)) for j in js for c in cs]

    work += columns_work(0) + columns_work(3) + columns_work(1) + columns_work(4)
    work += tile_work(0) + update_work((0, 3, 1, 4), (0,))
    work += tile_work(1) + update_work((0, 3), (1,)) + columns_work(2) + update_work((1, 4), (1,))
    work += update_work((2,), (0, 1)) + columns_work(5) + tile_work(2)
    early = max(at for kind, u, at in INNER + OUTER if kind == 1 and u < count)
    starts = [min(u for u in range(last) if UNITS[u][0] == r) for r in range(4)]

    def hooks(i):
        if i == 0:
            load_panel.wait()
        if i == 3:
            panel_copies[1].start()
            inv_line(0, "wait")
            inv_line(1, "start")
        if i == starts[1]:
            panel_copies[0].wait_recv()
            panel_copies[2].start()
        if i == starts[1] + 1:
            inv_line(1, "wait")
            inv_line(2, "start")
        if i == starts[2]:
            panel_copies[1].wait_recv()
            panel_copies[3].start()
        if i == starts[2] + 2:
            inv_line(2, "wait")
            inv_grid("start")
        if i == starts[3]:
            panel_copies[2].wait_recv()
            panel_copies[3].wait_recv()
        if i == early:
            for u in range(count):
                spread_tile(u)
        if i == last - 1:
            inv_grid("wait")
            inv_team("start")
        if i == last:
            inv_team("wait")
        if i == last + 5 * blocks:
            load_held.wait()

    def role_work(steps, functions, i):
        for kind, u, at in steps:
            if at == i:
                functions[kind](u)

    for i in range(len(work) + 1):
        if any(at == i for _, _, at in INNER):
            @pl.when(is_inner)
            def _():
                role_work(INNER, (middle, finished_inner, relay), i)

        if any(at == i for _, _, at in OUTER):
            @pl.when(is_outer)
            def _():
                role_work(OUTER, (None, finished_outer, relay), i)

        hooks(i)
        if i < len(work):
            function, at = work[i]
            function(*at)

    for copy in panel_copies:
        copy.wait_send()
    for s in range(lines - 1):
        inv_line(s, "drain")
    inv_grid("drain")
    inv_team("drain")
    for u in range(last):
        r, c = UNITS[u]
        k = slot_of(r, c)
        at = staged(r, c)
        ref = blk.at[place(team, r, c)]
        await_on(ref, team_send.at[u])

        @pl.when(is_outer)
        def _():
            await_on(outgoing.at[at], outer_send.at[u])

        @pl.when(is_inner)
        def _():
            await_on(outgoing.at[at], inner_send.at[u])
            await_on(ref, total_send.at[u])

        @pl.when(in_half(c) & sends_tile)
        def _():
            await_on(ref, tile_send.at[0, k])
            await_on(ref, tile_send.at[1, k])
            if u >= DIRECT:
                @pl.when(straight)
                def _():
                    await_on(ref, tile_send.at[3, k])

            @pl.when(team != owner)
            def _():
                await_on(ref, tile_send.at[2, k])

        @pl.when(relays(u))
        def _():
            for t in (0, 1):
                await_on(tile.at[tile_place(t, r, c)], relay_send.at[t, k])


def finish(cols, both, held, factor_part, factor_out, front_out, done, sems):
    count, side_pieces = cols.shape[0], both.shape[0]
    wide = cols.shape[2]
    near = (side_pieces - 1) * wide
    copies = [pltpu.make_async_copy(factor_part, factor_out, sems.at[0])]
    at = (pl.ds(0, near), pl.ds(0, (count - 1) * wide))
    copies.append(pltpu.make_async_copy(held.at[at], front_out.at[at], sems.at[1]))
    for copy in copies:
        copy.start()

    def update(j, c):
        rows, columns = slice(j * wide, (j + 1) * wide), slice(c * wide, (c + 1) * wide)
        change = contract_rows(both[j], cols[c])
        done[rows, columns] = held[rows, columns] - (change[:wide] + change[wide:])
        at = (pl.ds(j * wide, wide), pl.ds(c * wide, wide))
        copies.append(pltpu.make_async_copy(done.at[at], front_out.at[at], sems.at[len(copies)]))
        copies[-1].start()

    for j in range(side_pieces - 1):
        update(j, count - 1)
    for c in range(count):
        update(side_pieces - 1, c)
    for copy in copies:
        copy.wait()


def local_kernels(lines, grids, design_panel, design_front, arc_ids, arc_weight, row_counts, panel_inverse, front):
    bf16 = jnp.bfloat16
    slab, whole = panel_inverse.shape
    rows, width = design_panel.shape
    cols = design_front.shape[1]
    tile_rows = front.shape[0]
    side = whole // 2
    share = slab // 2
    wide = tile_rows // 3
    count = cols // wide
    vmem = pl.BlockSpec(memory_space=pltpu.VMEM)
    smem = pl.BlockSpec(memory_space=pltpu.SMEM)
    hbm = pl.BlockSpec(memory_space=pltpu.HBM)
    dma = pltpu.SemaphoreType.DMA
    hops = lines - 1
    arcs = arc_weight.shape[0]

    def stay(value):
        return pltpu.with_memory_space_constraint(value, pltpu.HBM)

    units = grids * count
    slots = units // 2
    f32 = jnp.float32
    outs = pl.pallas_call(
        exchange,
        out_shape=(
            jax.ShapeDtypeStruct((count, whole, wide), bf16),
            jax.ShapeDtypeStruct((3, whole, 2 * wide), bf16),
            jax.ShapeDtypeStruct(front.shape, f32),
            jax.ShapeDtypeStruct((slab, cols), f32),
        ),
        in_specs=[hbm, hbm, hbm, hbm, smem, hbm, hbm],
        out_specs=(vmem,) * 4,
        scratch_shapes=[
            pltpu.VMEM((count, whole, wide), bf16),
            pltpu.VMEM((3, whole, wide), bf16),
            pltpu.VMEM((2, lines, 2, share, side + 128), bf16),
            pltpu.VMEM((lines, 2, share, side), bf16),
            pltpu.VMEM((rows // arcs, arcs), jnp.int32),
            pltpu.VMEM((1, arcs), f32),
            pltpu.VMEM((slab, whole), f32),
            pltpu.VMEM((grids, rows, width), bf16),
            pltpu.VMEM((rows, cols), bf16),
            pltpu.VMEM((rows, arcs), f32),
            pltpu.VMEM((count, grids * width, wide), bf16),
            pltpu.VMEM((count, grids * width, wide), bf16),
            pltpu.VMEM((count, grids * width, wide), bf16),
            pltpu.VMEM((count, grids * width, wide), f32),
            dma((count,)), dma((5,)), dma((4,)), dma((4,)),
            dma((units,)), dma((units,)), dma((units,)), dma((units,)),
            dma((units,)), dma((units,)), dma((units,)), dma((units,)),
            dma((4, slots)), dma((2, slots)), dma((2, slots)),
            dma((3, 2, hops)), dma((3, 2, hops)), dma((3,)), dma((3,)), dma((3,)), dma((3,)),
        ],
        compiler_params=pltpu.CompilerParams(
            collective_id=0, has_side_effects=True, vmem_limit_bytes=30 * 2**20
        ),
        name="exchange",
    )(stay(design_panel), stay(design_front), stay(arc_ids.reshape((rows // arcs, arcs))),
      stay(arc_weight[None, :]), row_counts, stay(panel_inverse), stay(front))
    return pl.pallas_call(
        finish,
        out_shape=(
            jax.ShapeDtypeStruct((slab, cols), f32),
            jax.ShapeDtypeStruct(front.shape, f32),
        ),
        in_specs=[vmem] * 4,
        out_specs=(hbm, hbm),
        scratch_shapes=[
            pltpu.VMEM(front.shape, f32),
            dma((count + 4,)),
        ],
        compiler_params=pltpu.CompilerParams(vmem_limit_bytes=12 * 2**20),
        name="finish",
    )(*outs)


def solution(mesh):
    placed = (
        P("obs", ("team", "grid")),
        P("obs", "grid"),
        P("obs"),
        P(),
        P("obs"),
        P(("team", "obs"), None),
        P(("team", "obs"), "grid"),
    )
    sizes = mesh.shape
    fits = sizes["team"] == 2 and sizes["obs"] == 4 and sizes["grid"] == 4
    return jax.shard_map(
        functools.partial(local_kernels, sizes["obs"], sizes["grid"]) if fits else local,
        mesh=mesh,
        in_specs=placed,
        out_specs=(P(("team", "obs"), "grid"), P(("team", "obs"), "grid")),
        check_vma=False,
    )
```

```python
import functools

import jax
import jax.numpy as jnp
from jax import lax
from jax.experimental import pallas as pl
from jax.experimental.pallas import tpu as pltpu
from jax.sharding import PartitionSpec as P


def live_weights(arc_ids, arc_weight, row_counts):
    row_total = arc_ids.shape[0]
    arc_total = arc_weight.shape[0]
    hit = arc_ids[:, None] == lax.broadcasted_iota(jnp.int32, (row_total, arc_total), 1)
    looked = jnp.sum(jnp.where(hit, arc_weight[None, :], 0.0), axis=1)
    is_live = lax.broadcasted_iota(jnp.int32, (row_total,), 0) < row_counts[0]
    return looked * is_live.astype(jnp.float32)


def contract_rows(left, right):
    return lax.dot_general(
        left, right, (((0,), (0,)), ((), ())), preferred_element_type=jnp.float32
    )


def local(design_panel, design_front, arc_ids, arc_weight, row_counts, panel_inverse, front):
    high = lax.reduce_precision(panel_inverse, 8, 7)
    split = jnp.concatenate([high, panel_inverse - high], axis=1).astype(jnp.bfloat16)
    inverse_whole = lax.all_gather(split, ("team", "obs"), axis=0, tiled=True)
    weights = live_weights(arc_ids, arc_weight, row_counts)
    scaled_front = (design_front.astype(jnp.float32) * weights[:, None]).astype(jnp.bfloat16)
    panel_piece = lax.all_gather(design_panel, "grid", axis=1, tiled=True)
    partial_value = contract_rows(panel_piece, scaled_front)
    slab_rows = panel_inverse.shape[0]
    place_index = lax.axis_index(("team", "obs"))
    block_part = lax.psum_scatter(partial_value, "obs", scatter_dimension=0, tiled=True)
    block_part = block_part.astype(jnp.bfloat16)
    block_whole = lax.all_gather(block_part, ("team", "obs"), axis=0, tiled=True)
    factor_cols = jnp.dot(
        inverse_whole,
        jnp.concatenate([block_whole, block_whole], axis=0),
        preferred_element_type=jnp.float32,
    )
    factor_part = lax.dynamic_slice_in_dim(factor_cols, place_index * slab_rows, slab_rows, 0)
    factor_cols = factor_cols.astype(jnp.bfloat16)
    tile_rows = front.shape[0]
    tile_ratio = factor_cols.shape[1] // tile_rows
    offset = place_index % tile_ratio * tile_rows
    own_slice = lax.dynamic_slice_in_dim(factor_cols, offset, tile_rows, 1)
    kept = jnp.where(lax.axis_index("grid") == place_index // tile_ratio, own_slice, 0)
    factor_rows = lax.psum(kept.astype(jnp.bfloat16), "grid")
    return (factor_part, front - contract_rows(factor_rows, factor_cols))


MESH = pl.DeviceIdType.MESH


DIRECT = 18
UNITS = (
    (0, 0), (0, 3), (0, 1), (0, 4), (0, 2), (0, 5), (1, 0), (1, 3), (1, 1), (1, 4), (2, 0), (2, 3), (2, 1),
    (2, 4), (3, 0), (3, 3), (3, 1), (3, 4), (1, 2), (2, 2), (3, 2), (1, 5), (2, 5), (3, 5)
)
INNER = (
    (0, 0, 5), (0, 1, 6), (0, 2, 6), (0, 3, 8), (0, 4, 10), (1, 0, 10), (0, 5, 10), (1, 1, 10), (0, 6, 11),
    (1, 2, 11), (0, 7, 12), (1, 3, 12), (0, 8, 14), (1, 4, 14), (0, 9, 14), (1, 5, 14), (0, 10, 14), (1, 6,
    14), (0, 11, 15), (1, 7, 15), (0, 12, 17), (1, 8, 17), (0, 13, 18), (1, 9, 18), (0, 14, 20), (1, 10, 20),
    (2, 0, 21), (0, 15, 21), (1, 11, 21), (2, 1, 21), (2, 2, 22), (2, 3, 22), (0, 16, 22), (1, 12, 22), (2, 4,
    23), (2, 5, 23), (0, 17, 24), (1, 13, 24), (2, 6, 24), (2, 7, 24), (0, 18, 24), (1, 14, 24), (2, 8, 24),
    (2, 9, 24), (0, 19, 24), (1, 15, 24), (2, 10, 27), (2, 11, 27), (0, 20, 28), (1, 16, 28), (2, 12, 29), (0,
    21, 31), (1, 17, 31), (2, 13, 31), (2, 14, 34), (0, 22, 35), (1, 18, 35), (2, 15, 37), (0, 23, 38), (1,
    19, 38), (2, 16, 40), (1, 20, 40), (2, 17, 40), (1, 21, 40), (1, 22, 40), (2, 18, 40), (2, 19, 43), (1,
    23, 45), (2, 20, 45), (2, 21, 45), (2, 22, 45), (2, 23, 50)
)
OUTER = (
    (1, 0, 14), (1, 1, 14), (1, 2, 14), (1, 3, 15), (1, 4, 18), (1, 5, 20), (1, 6, 22), (2, 0, 23), (2, 1,
    23), (1, 7, 23), (2, 2, 24), (2, 3, 24), (1, 8, 24), (2, 4, 24), (2, 5, 24), (1, 9, 24), (2, 6, 24), (1,
    10, 24), (2, 7, 24), (1, 11, 24), (2, 8, 24), (1, 12, 24), (2, 9, 24), (1, 13, 24), (2, 10, 24), (1, 14,
    24), (2, 11, 24), (1, 15, 24), (2, 12, 27), (1, 16, 29), (2, 13, 32), (1, 17, 32), (2, 14, 35), (1, 18,
    37), (2, 15, 40), (1, 19, 40), (2, 16, 40), (1, 20, 40), (2, 17, 40), (1, 21, 40), (1, 22, 40), (2, 18,
    42), (1, 23, 44), (2, 19, 45), (2, 20, 45), (2, 21, 45), (2, 22, 45), (2, 23, 49)
)


def exchange(
    panel, front_cols, ids_hbm, arc_hbm, counts, inverse_hbm, front,
    cols, both, held, factor_part,
    blk, tile, inv_diag, inv_off, ids, arc_weight, inverse_rows,
    panels, scaled, weights, outgoing, from_outer, from_inner, own,
    front_sem, local_sem, panel_send, panel_recv, outer_send, outer_recv, inner_send, inner_recv,
    total_send, total_recv, team_send, team_recv, tile_send, relay_send, tile_recv,
    inv_line_send, inv_line_recv, inv_grid_send, inv_grid_recv, inv_team_send, inv_team_recv,
):
    team, z, grid = lax.axis_index("team"), lax.axis_index("obs"), lax.axis_index("grid")
    rows, width = panel.shape
    lines = inv_diag.shape[1]
    share = inv_diag.shape[3]
    side = inv_off.shape[3]
    x, y = lax.rem(grid, 2), lax.div(grid, 2)
    beside_x = y * 2 + (1 - x)
    beside_y = (1 - y) * 2 + x
    across = (1 - y) * 2 + (1 - x)
    partner = 1 - team
    is_inner = (z == 1) | (z == 2)
    is_outer = jnp.logical_not(is_inner)
    mate = jnp.where(z < 2, 1 - z, 5 - z)
    other = jnp.clip(3 - z, 1, 2)
    half = lax.rem(z, 2)
    root_x = lax.div(z, 2)
    owner = y
    sends_tile = x == root_x
    root_y = team
    at_x = (x != root_x) & (y == root_y)
    straight = root_x == 0

    barrier = pltpu.get_barrier_semaphore()
    for where in (
        {"grid": beside_x}, {"grid": beside_y}, {"team": partner}, {"obs": mate},
        {"team": partner, "grid": beside_x}, {"team": partner, "grid": beside_y},
        {"grid": across}, {"team": partner, "grid": across},
    ):
        pl.semaphore_signal(barrier, inc=1, device_id=where, device_id_type=MESH)

    @pl.when(is_inner)
    def _():
        pl.semaphore_signal(barrier, inc=1, device_id={"obs": other}, device_id_type=MESH)

    count, side_pieces = blk.shape[0], tile.shape[0]
    wide = blk.shape[2]

    def load_front(c):
        at = (slice(None), pl.ds(c * wide, wide))
        return pltpu.make_async_copy(front_cols.at[at], scaled.at[at], front_sem.at[c])

    load_inverse = pltpu.make_async_copy(inverse_hbm, inverse_rows, local_sem.at[0])
    load_ids = pltpu.make_async_copy(ids_hbm, ids, local_sem.at[1])
    load_arcs = pltpu.make_async_copy(arc_hbm, arc_weight, local_sem.at[2])
    load_panel = pltpu.make_async_copy(panel, panels.at[0], local_sem.at[3])
    load_held = pltpu.make_async_copy(front, held, local_sem.at[4])
    load_inverse.start()
    load_ids.start()
    load_arcs.start()
    load_front(0).start()
    load_panel.start()
    for r, c in UNITS[1:count]:
        load_front(c).start()
    load_held.start()

    step = rows // 8
    load_inverse.wait()
    pair_at = jnp.where(team == 0, x, y)
    mine = inverse_rows[pl.ds(pl.multiple_of(pair_at * share, share), share), :]
    rounded = mine.astype(jnp.bfloat16)
    row_at = lax.broadcasted_iota(jnp.int32, mine.shape, 0) + (team * side + z * width + pair_at * share)
    on_diagonal = lax.broadcasted_iota(jnp.int32, mine.shape, 1) == row_at
    rest = jnp.sum(jnp.where(on_diagonal, mine - rounded.astype(jnp.float32), 0.0), axis=1, keepdims=True)
    rest = jnp.broadcast_to(rest, (share, inv_diag.shape[4] - side)).astype(jnp.bfloat16)

    @pl.when(team == 0)
    def _():
        inv_diag[0, z, pair_at, :, :side] = rounded[:, :side]

    @pl.when(team == 1)
    def _():
        inv_diag[1, z, pair_at, :, :side] = rounded[:, side:]
        inv_off[z, pair_at] = rounded[:, :side]

    inv_diag[team, z, pair_at, :, side:] = rest

    pl.semaphore_wait(barrier, jnp.where(is_inner, 9, 8))

    def remote(src, dst, send, recv, where):
        return pltpu.make_async_remote_copy(
            src_ref=src, dst_ref=dst, send_sem=send, recv_sem=recv,
            device_id=where, device_id_type=MESH,
        )

    def await_on(ref, sem):
        pltpu.make_async_copy(ref, ref, sem).wait()

    first = jnp.where(team == 0, beside_x, beside_y)
    second = jnp.where(team == 0, beside_y, beside_x)
    top, bottom = pl.ds(0, rows // 2), pl.ds(rows // 2, rows // 2)
    panel_copies = [
        remote(panel, panels.at[1], panel_send.at[0], panel_recv.at[0], {"grid": first}),
        remote(panel, panels.at[2], panel_send.at[1], panel_recv.at[1], {"grid": second}),
        remote(panels.at[1, top], panels.at[3, top], panel_send.at[2], panel_recv.at[2], {"grid": second}),
        remote(panels.at[2, bottom], panels.at[3, bottom], panel_send.at[3], panel_recv.at[3], {"grid": first}),
    ]
    panel_copies[0].start()

    inv_parts = (
        (0, team == 0, lambda *at: inv_diag.at[(0,) + at]),
        (1, team == 1, lambda *at: inv_diag.at[(1,) + at]),
        (2, team == 1, lambda *at: inv_off.at[at]),
    )

    def inv_line(s, what):
        for k, has, of in inv_parts:
            for d, hop in ((0, 1), (1, -1)):
                held = z - hop * s
                sends = (held >= 0) & (held < lines) & (z + hop >= 0) & (z + hop < lines)
                came = z - hop * (s + 1)
                comes = (came >= 0) & (came < lines)
                if what == "start":
                    @pl.when(has & sends)
                    def _():
                        ref = of(jnp.clip(held, 0, lines - 1), pair_at)
                        remote(ref, ref, inv_line_send.at[k, d, s], inv_line_recv.at[k, d, s],
                               {"obs": jnp.clip(z + hop, 0, lines - 1)}).start()
                elif what == "wait":
                    @pl.when(has & comes)
                    def _():
                        await_on(of(jnp.clip(came, 0, lines - 1), pair_at), inv_line_recv.at[k, d, s])
                else:
                    @pl.when(has & sends)
                    def _():
                        await_on(of(jnp.clip(held, 0, lines - 1), pair_at), inv_line_send.at[k, d, s])

    def inv_grid(what):
        every = pl.ds(0, lines)
        for k, has, of in inv_parts:
            @pl.when(has)
            def _():
                sent, came = of(every, pair_at), of(every, 1 - pair_at)
                if what == "start":
                    remote(sent, sent, inv_grid_send.at[k], inv_grid_recv.at[k], {"grid": first}).start()
                elif what == "wait":
                    await_on(came, inv_grid_recv.at[k])
                else:
                    await_on(sent, inv_grid_send.at[k])

    def inv_team(what):
        for k, has, of in inv_parts:
            @pl.when(has)
            def _():
                if what == "start":
                    remote(of(), of(), inv_team_send.at[k], inv_team_recv.at[k], {"team": partner}).start()
                elif what == "drain":
                    await_on(of(), inv_team_send.at[k])

            if what == "wait":
                @pl.when(jnp.logical_not(has))
                def _():
                    await_on(of(), inv_team_recv.at[k])

    inv_line(0, "start")

    arcs = arc_weight.shape[1]
    live = counts[0]
    load_ids.wait()
    load_arcs.wait()
    lane = lax.broadcasted_iota(jnp.int32, (arcs, arcs), 1)
    place_of = lax.broadcasted_iota(jnp.int32, (arcs, arcs), 0)

    def upright(line):
        return jnp.sum(jnp.where(lane == place_of, line, 0), axis=1, keepdims=True)

    arc_column = upright(arc_weight[...])
    for i in range(rows // arcs):
        hit = ids[i:i + 1, :] == place_of
        looked = jnp.sum(jnp.where(hit, arc_column, 0.0), axis=0, keepdims=True)
        slot = lax.broadcasted_iota(jnp.int32, (1, arcs), 1) + i * arcs
        weights[i * arcs:(i + 1) * arcs, :] = jnp.broadcast_to(upright(jnp.where(slot < live, looked, 0.0)), (arcs, arcs))

    def scale(c):
        at_cols = slice(c * wide, (c + 1) * wide)
        load_front(c).wait()

        @pl.loop(0, rows // step)
        def _(i):
            at = pl.ds(pl.multiple_of(i * step, step), step)
            factor = jnp.concatenate([weights[at, :]] * (wide // weights.shape[1]), axis=1)
            part = scaled[at, at_cols].astype(jnp.float32)
            scaled[at, at_cols] = (part * factor).astype(jnp.bfloat16)

    def source(t, r):
        if r == 0:
            return grid
        if r == 3:
            return across
        return jnp.where(t == r - 1, beside_x, beside_y)

    def tile_source(t, r):
        root = root_y * 2 + root_x
        flip_x = root_y * 2 + (1 - root_x)
        flip_y = (1 - root_y) * 2 + root_x
        both = (1 - root_y) * 2 + (1 - root_x)
        return (root, (flip_x, flip_y)[t], (flip_y, flip_x)[t], both)[r]

    def staged(r, c):
        return c, pl.ds(r * width, width)

    def block_rows(t, g):
        return pl.ds(pl.multiple_of((t * 4 + g) * width, width), width)

    def place(t, r, c):
        return c, block_rows(t, source(t, r))

    def tile_place(t, r, c):
        return c % side_pieces, block_rows(t, tile_source(t, r))

    def slot_of(r, c):
        return r * side_pieces + c % side_pieces

    def in_half(c):
        return half == c // side_pieces

    def relays(u):
        stored = at_x & in_half(UNITS[u][1])
        return stored & jnp.logical_not(straight) if u >= DIRECT else stored

    def compute(u):
        r, c = UNITS[u]
        if r == 0:
            scale(c)
        total = contract_rows(panels[r], scaled[:, c * wide:(c + 1) * wide])
        at = staged(r, c)

        @pl.when(is_inner)
        def _():
            own[at] = total

        @pl.when(is_outer)
        def _():
            outgoing[at] = total.astype(jnp.bfloat16)
            remote(outgoing.at[at], from_outer.at[at], outer_send.at[u], outer_recv.at[u], {"obs": mate}).start()

    def middle(u):
        at = staged(*UNITS[u])
        await_on(from_outer.at[at], outer_recv.at[u])
        total = own[at] + from_outer[at].astype(jnp.float32)
        own[at] = total
        outgoing[at] = total.astype(jnp.bfloat16)
        remote(outgoing.at[at], from_inner.at[at], inner_send.at[u], inner_recv.at[u], {"obs": other}).start()

    def spread_tile(u):
        r, c = UNITS[u]
        ref = blk.at[place(team, r, c)]

        @pl.when(sends_tile & in_half(c))
        def _():
            k = slot_of(r, c)
            to = tile.at[c % side_pieces, block_rows(team, source(team, r))]
            remote(ref, to, tile_send.at[0, k], tile_recv.at[team, k], {"team": owner, "grid": beside_x}).start()
            remote(ref, to, tile_send.at[1, k], tile_recv.at[team, k], {"team": owner, "grid": beside_y}).start()
            if u >= DIRECT:
                @pl.when(straight)
                def _():
                    remote(ref, to, tile_send.at[3, k], tile_recv.at[team, k], {"team": owner, "grid": across}).start()

            @pl.when(team == owner)
            def _():
                pltpu.make_async_copy(ref, to, tile_recv.at[team, k]).start()

            @pl.when(team != owner)
            def _():
                remote(ref, to, tile_send.at[2, k], tile_recv.at[team, k], {"team": partner}).start()

    def spread(u):
        ref = blk.at[place(team, *UNITS[u])]
        if u >= count:
            spread_tile(u)
        remote(ref, ref, team_send.at[u], team_recv.at[u], {"team": partner}).start()

    def finished_inner(u):
        r, c = UNITS[u]
        at = staged(r, c)
        await_on(from_inner.at[at], inner_recv.at[u])
        total = own[at] + from_inner[at].astype(jnp.float32)
        spot = place(team, r, c)
        blk[spot] = total.astype(jnp.bfloat16)
        ref = blk.at[spot]
        remote(ref, ref, total_send.at[u], total_recv.at[u], {"obs": mate}).start()
        spread(u)

    def finished_outer(u):
        await_on(blk.at[place(team, *UNITS[u])], total_recv.at[u])
        spread(u)

    def relay(u):
        r, c = UNITS[u]
        k = slot_of(r, c)

        @pl.when(relays(u))
        def _():
            for t in (0, 1):
                ref = tile.at[tile_place(t, r, c)]
                await_on(ref, tile_recv.at[t, k])
                remote(ref, ref, relay_send.at[t, k], tile_recv.at[t, k], {"grid": beside_y}).start()

    slab = inverse_rows.shape[0]
    size = 2 * slab
    blocks = blk.shape[1] // size
    pair = team * lines + z

    def factor_of(ref, c, t):
        middle_row, begin = side // 2, t * side
        near = inv_diag[t].reshape((side, inv_diag.shape[4]))
        total = near[:, side:side + 1].astype(jnp.float32) * ref[c, begin:begin + side].astype(jnp.float32)
        total += jnp.dot(
            near[:, :middle_row], ref[c, begin:begin + middle_row], preferred_element_type=jnp.float32
        )
        if t:
            total += jnp.dot(
                inv_off[...].reshape((side, side)), ref[c, :side], preferred_element_type=jnp.float32
            )
        lower = total[middle_row:] + jnp.dot(
            near[middle_row:, middle_row:side], ref[c, begin + middle_row:begin + side],
            preferred_element_type=jnp.float32,
        )
        return total[:middle_row], lower

    def factor_columns(c, r):
        if r == 0:
            for u in range(len(UNITS)):
                if UNITS[u][1] == c:
                    await_on(blk.at[place(partner, *UNITS[u])], team_recv.at[u])
        if r % 2 == 0:
            return
        for k, value in enumerate(factor_of(blk, c, r // 2), r - 1):
            cols[c, k * size:(k + 1) * size] = value.astype(jnp.bfloat16)
            for part in range(size // slab):
                @pl.when(pair == k * (size // slab) + part)
                def _():
                    factor_part[:, c * wide:(c + 1) * wide] = value[part * slab:(part + 1) * slab]

    def factor_tile(j, r):
        if r == 0:
            for u, (d, c) in enumerate(UNITS):
                if c % side_pieces == j:
                    @pl.when(in_half(c) & jnp.logical_not(relays(u)))
                    def _():
                        for t in (0, 1):
                            await_on(tile.at[tile_place(t, d, c)], tile_recv.at[t, slot_of(d, c)])
        if r % 2 == 0:
            return
        for k, value in enumerate(factor_of(tile, j, r // 2), r - 1):
            upper = value.astype(jnp.bfloat16)
            both[j, k * size:(k + 1) * size, :wide] = upper
            both[j, k * size:(k + 1) * size, wide:] = (value - upper.astype(jnp.float32)).astype(jnp.bfloat16)

    def update(c, j):
        near, at = slice(j * wide, (j + 1) * wide), slice(c * wide, (c + 1) * wide)
        change = contract_rows(both[j], cols[c])
        held[near, at] = held[near, at] - (change[:wide] + change[wide:])

    last = len(UNITS)
    work = [(compute, (u,)) for u in range(last)]

    def columns_work(c):
        return [(factor_columns, (c, r)) for r in range(blocks)]

    def tile_work(j):
        return [(factor_tile, (j, r)) for r in range(blocks)]

    def update_work(cs, js):
        return [(update, (c, j)) for j in js for c in cs]

    work += columns_work(0) + columns_work(3) + columns_work(1) + columns_work(4)
    work += tile_work(0) + update_work((0, 3, 1, 4), (0,))
    work += tile_work(1) + update_work((0, 3), (1,)) + columns_work(2) + update_work((1, 4), (1,))
    work += update_work((2,), (0, 1)) + columns_work(5) + tile_work(2)
    early = max(at for kind, u, at in INNER + OUTER if kind == 1 and u < count)
    starts = [min(u for u in range(last) if UNITS[u][0] == r) for r in range(4)]

    def hooks(i):
        if i == 0:
            load_panel.wait()
        if i == 3:
            panel_copies[1].start()
            inv_line(0, "wait")
            inv_line(1, "start")
        if i == starts[1]:
            panel_copies[0].wait_recv()
            panel_copies[2].start()
        if i == starts[1] + 1:
            inv_line(1, "wait")
            inv_line(2, "start")
        if i == starts[2]:
            panel_copies[1].wait_recv()
            panel_copies[3].start()
        if i == starts[2] + 2:
            inv_line(2, "wait")
            inv_grid("start")
        if i == starts[3]:
            panel_copies[2].wait_recv()
            panel_copies[3].wait_recv()
        if i == early:
            for u in range(count):
                spread_tile(u)
        if i == last - 1:
            inv_grid("wait")
            inv_team("start")
        if i == last:
            inv_team("wait")
        if i == last + 5 * blocks:
            load_held.wait()

    def role_work(steps, functions, i):
        for kind, u, at in steps:
            if at == i:
                functions[kind](u)

    for i in range(len(work) + 1):
        if any(at == i for _, _, at in INNER):
            @pl.when(is_inner)
            def _():
                role_work(INNER, (middle, finished_inner, relay), i)

        if any(at == i for _, _, at in OUTER):
            @pl.when(is_outer)
            def _():
                role_work(OUTER, (None, finished_outer, relay), i)

        hooks(i)
        if i < len(work):
            function, at = work[i]
            function(*at)

    for copy in panel_copies:
        copy.wait_send()
    for s in range(lines - 1):
        inv_line(s, "drain")
    inv_grid("drain")
    inv_team("drain")
    for u in range(last):
        r, c = UNITS[u]
        k = slot_of(r, c)
        at = staged(r, c)
        ref = blk.at[place(team, r, c)]
        await_on(ref, team_send.at[u])

        @pl.when(is_outer)
        def _():
            await_on(outgoing.at[at], outer_send.at[u])

        @pl.when(is_inner)
        def _():
            await_on(outgoing.at[at], inner_send.at[u])
            await_on(ref, total_send.at[u])

        @pl.when(in_half(c) & sends_tile)
        def _():
            await_on(ref, tile_send.at[0, k])
            await_on(ref, tile_send.at[1, k])
            if u >= DIRECT:
                @pl.when(straight)
                def _():
                    await_on(ref, tile_send.at[3, k])

            @pl.when(team != owner)
            def _():
                await_on(ref, tile_send.at[2, k])

        @pl.when(relays(u))
        def _():
            for t in (0, 1):
                await_on(tile.at[tile_place(t, r, c)], relay_send.at[t, k])


def finish(cols, both, held, factor_part, factor_out, front_out, done, sems):
    count, side_pieces = cols.shape[0], both.shape[0]
    wide = cols.shape[2]
    near = (side_pieces - 1) * wide
    copies = [pltpu.make_async_copy(factor_part, factor_out, sems.at[0])]
    at = (pl.ds(0, near), pl.ds(0, (count - 1) * wide))
    copies.append(pltpu.make_async_copy(held.at[at], front_out.at[at], sems.at[1]))
    for copy in copies:
        copy.start()

    def update(j, c):
        rows, columns = slice(j * wide, (j + 1) * wide), slice(c * wide, (c + 1) * wide)
        change = contract_rows(both[j], cols[c])
        done[rows, columns] = held[rows, columns] - (change[:wide] + change[wide:])
        at = (pl.ds(j * wide, wide), pl.ds(c * wide, wide))
        copies.append(pltpu.make_async_copy(done.at[at], front_out.at[at], sems.at[len(copies)]))
        copies[-1].start()

    for j in range(side_pieces - 1):
        update(j, count - 1)
    for c in range(count):
        update(side_pieces - 1, c)
    for copy in copies:
        copy.wait()


def local_kernels(lines, grids, design_panel, design_front, arc_ids, arc_weight, row_counts, panel_inverse, front):
    bf16 = jnp.bfloat16
    slab, whole = panel_inverse.shape
    rows, width = design_panel.shape
    cols = design_front.shape[1]
    tile_rows = front.shape[0]
    side = whole // 2
    share = slab // 2
    wide = tile_rows // 3
    count = cols // wide
    vmem = pl.BlockSpec(memory_space=pltpu.VMEM)
    smem = pl.BlockSpec(memory_space=pltpu.SMEM)
    hbm = pl.BlockSpec(memory_space=pltpu.HBM)
    dma = pltpu.SemaphoreType.DMA
    hops = lines - 1
    arcs = arc_weight.shape[0]

    def stay(value):
        return pltpu.with_memory_space_constraint(value, pltpu.HBM)

    units = grids * count
    slots = units // 2
    f32 = jnp.float32
    outs = pl.pallas_call(
        exchange,
        out_shape=(
            jax.ShapeDtypeStruct((count, whole, wide), bf16),
            jax.ShapeDtypeStruct((3, whole, 2 * wide), bf16),
            jax.ShapeDtypeStruct(front.shape, f32),
            jax.ShapeDtypeStruct((slab, cols), f32),
        ),
        in_specs=[hbm, hbm, hbm, hbm, smem, hbm, hbm],
        out_specs=(vmem,) * 4,
        scratch_shapes=[
            pltpu.VMEM((count, whole, wide), bf16),
            pltpu.VMEM((3, whole, wide), bf16),
            pltpu.VMEM((2, lines, 2, share, side + 128), bf16),
            pltpu.VMEM((lines, 2, share, side), bf16),
            pltpu.VMEM((rows // arcs, arcs), jnp.int32),
            pltpu.VMEM((1, arcs), f32),
            pltpu.VMEM((slab, whole), f32),
            pltpu.VMEM((grids, rows, width), bf16),
            pltpu.VMEM((rows, cols), bf16),
            pltpu.VMEM((rows, arcs), f32),
            pltpu.VMEM((count, grids * width, wide), bf16),
            pltpu.VMEM((count, grids * width, wide), bf16),
            pltpu.VMEM((count, grids * width, wide), bf16),
            pltpu.VMEM((count, grids * width, wide), f32),
            dma((count,)), dma((5,)), dma((4,)), dma((4,)),
            dma((units,)), dma((units,)), dma((units,)), dma((units,)),
            dma((units,)), dma((units,)), dma((units,)), dma((units,)),
            dma((4, slots)), dma((2, slots)), dma((2, slots)),
            dma((3, 2, hops)), dma((3, 2, hops)), dma((3,)), dma((3,)), dma((3,)), dma((3,)),
        ],
        compiler_params=pltpu.CompilerParams(
            collective_id=0, has_side_effects=True, vmem_limit_bytes=30 * 2**20
        ),
        name="exchange",
    )(stay(design_panel), stay(design_front), stay(arc_ids.reshape((rows // arcs, arcs))),
      stay(arc_weight[None, :]), row_counts, stay(panel_inverse), stay(front))
    return pl.pallas_call(
        finish,
        out_shape=(
            jax.ShapeDtypeStruct((slab, cols), f32),
            jax.ShapeDtypeStruct(front.shape, f32),
        ),
        in_specs=[vmem] * 4,
        out_specs=(hbm, hbm),
        scratch_shapes=[
            pltpu.VMEM(front.shape, f32),
            dma((count + 4,)),
        ],
        compiler_params=pltpu.CompilerParams(vmem_limit_bytes=12 * 2**20),
        name="finish",
    )(*outs)


def solution(mesh):
    placed = (
        P("obs", ("team", "grid")),
        P("obs", "grid"),
        P("obs"),
        P(),
        P("obs"),
        P(("team", "obs"), None),
        P(("team", "obs"), "grid"),
    )
    sizes = mesh.shape
    fits = sizes["team"] == 2 and sizes["obs"] == 4 and sizes["grid"] == 4
    return jax.shard_map(
        functools.partial(local_kernels, sizes["obs"], sizes["grid"]) if fits else local,
        mesh=mesh,
        in_specs=placed,
        out_specs=(P(("team", "obs"), "grid"), P(("team", "obs"), "grid")),
        check_vma=False,
    )
```
